32 devices in a mesh: snap: 8 (over z, x), feat: 4 (over y, core).
Axes of the slice: x: 2, y: 2, z: 4, core: 2. Of those that a mesh axis runs over, the one named last changes fastest.
Arguments:
- node_features: bfloat16 [16, 512, 256], P('snap', None, 'feat'), may hold values from -6 to 6
- tile_rows: int32 [16, 8], P('snap'), may hold values from 0 to 3
- tile_cols: int32 [16, 8], P('snap'), may hold values from 0 to 3, as said below
- tile_counts: int32 [16], P('snap'), may hold values from 4 to 8, as said below
- tile_values: bfloat16 [16, 8, 128, 128], P('snap'), may hold values from -0.5 to 0.5
- layer_one: bfloat16 [256, 256], replicated, may hold values from -0.375 to 0.375
- layer_two: bfloat16 [256, 256], replicated, may hold values from -0.375 to 0.375
- query_weight: bfloat16 [256, 256], replicated, may hold values from -1.25 to 1.25
- key_weight: bfloat16 [256, 256], replicated, may hold values from -1.25 to 1.25
- value_weight: bfloat16 [256, 256], replicated, may hold values from -0.375 to 0.375
- out_weight: bfloat16 [256, 256], replicated, may hold values from -0.375 to 0.375
Outputs:
- evolved: bfloat16 [16, 512, 256], P('snap', None, 'feat')
The draws below stay inside these ranges and needn't reach their ends.
Inputs may be any that keep to these rules, and one draw needn't show every extreme that they name: `tile_cols`: block columns of the tile slots; a coordinate pair may be listed more than once, and such tiles add. `tile_counts`: some snapshot uses all 8 slots.
All inputs are finite; a program needn't handle non-finite values.
Results may differ from the reference program's by a relative error of at most 0.02.
The reference program's roundings to bfloat16 on the way count: a program that leaves them out, or rounds other values in their place, can miss the bound.
Values may be sent and summed in bfloat16 or wider, within the bound.
A program may use at most 64 MiB of HBM per device.

```python
import jax
import jax.numpy as jnp
from jax import lax

D = 256
HEADS = 8
TILE = 128
HEAD_DIM = 32
SNAPS = 16
VERT = 512
BLOCKS = 4
MAXT = 8
N_SNAP = 8


def tile_lists(key):
    row_ids = jax.random.randint(jax.random.fold_in(key, 101), (SNAPS, MAXT), 0, BLOCKS)
    col_ids = jax.random.randint(jax.random.fold_in(key, 102), (SNAPS, MAXT), 0, BLOCKS)
    levels = jax.random.randint(jax.random.fold_in(key, 103), (SNAPS,), 0, 11)
    counts = 4 + (MAXT - 4) * levels * levels * levels // 1000
    full_snapshot = jax.random.randint(jax.random.fold_in(key, 104), (), 0, SNAPS)
    counts = jnp.where(jnp.arange(SNAPS) == full_snapshot, MAXT, counts)
    return (row_ids.astype(jnp.int32), col_ids.astype(jnp.int32), counts.astype(jnp.int32))


def draw_tile_rows(key, part):
    return tile_lists(key)[0]


def draw_tile_cols(key, part):
    return tile_lists(key)[1]


def draw_tile_counts(key, part):
    return tile_lists(key)[2]


def attention_pair(key, which):
    separate = jnp.clip(jax.random.normal(jax.random.fold_in(key, 202 + which), (D, D), jnp.float32), -5.0, 5.0)
    combined = separate
    return (combined * D ** (-0.5)).astype(jnp.bfloat16)


def draw_query_weight(key, part):
    return attention_pair(key, 0)


def draw_key_weight(key, part):
    return attention_pair(key, 1)


def block_scale(rng, dims, split, smallest, largest):
    loudness = 1.0
    for axis_at, shards_of in split:
        draws = jax.random.uniform(jax.random.fold_in(jax.random.fold_in(rng, 6), axis_at), (shards_of,), jnp.float32, smallest / len(split), largest / len(split))
        loudness = loudness * jnp.repeat(jnp.exp(draws), dims[axis_at] // shards_of).reshape((-1,) + (1,) * (len(dims) - 1 - axis_at))
    return loudness


def normal_values(key, extent, spread, limit, split=(), kind=jnp.bfloat16):
    array = spread * jax.random.normal(key, extent, jnp.float32)
    if split:
        array = array * block_scale(key, extent, split, -0.22, 0.18)
    return jnp.clip(array, -limit, limit).astype(kind)


def setup_inputs(seed: int = 0) -> dict:
    splits = jax.random.split(jax.random.key(seed), 12)
    return {
        "node_features": normal_values(splits[0], (SNAPS, VERT, D), 1.0, 6.0, ((0, 8), (2, 4))),
        "tile_rows": draw_tile_rows(jax.random.fold_in(splits[11], 71), 0),
        "tile_cols": draw_tile_cols(jax.random.fold_in(splits[11], 71), 0),
        "tile_counts": draw_tile_counts(jax.random.fold_in(splits[11], 71), 0),
        "tile_values": normal_values(splits[4], (SNAPS, MAXT, TILE, TILE), TILE ** -0.5, 0.5, ((0, 8),)),
        "layer_one": normal_values(splits[5], (D, D), D ** -0.5, 0.375),
        "layer_two": normal_values(splits[6], (D, D), D ** -0.5, 0.375),
        "query_weight": draw_query_weight(jax.random.fold_in(splits[11], 71), 0),
        "key_weight": draw_key_weight(jax.random.fold_in(splits[11], 71), 0),
        "value_weight": normal_values(splits[9], (D, D), D ** -0.5, 0.375),
        "out_weight": normal_values(splits[10], (D, D), D ** -0.5, 0.375),
    }


masked_score = -1.0e30


def spread_snapshot(features, tile_block, block_rows, block_cols, slot_count):
    feat_width = features.shape[1]
    blocked = features.reshape(BLOCKS, TILE, feat_width)
    picked_blocks = blocked[block_cols]
    live_slots = (jnp.arange(MAXT, dtype=jnp.int32) < slot_count)
    products = jnp.einsum("irc,icf->irf", tile_block.astype(jnp.float32), picked_blocks.astype(jnp.float32), precision=lax.Precision.HIGHEST)
    products = products * live_slots.astype(jnp.float32)[:, None, None]
    membership = ((block_rows[None, :] == jnp.arange(BLOCKS, dtype=jnp.int32)[:, None]) & live_slots[None, :]).astype(jnp.float32)
    summed = jnp.dot(membership, products.reshape(MAXT, TILE * feat_width), precision=lax.Precision.HIGHEST)
    return summed.reshape(VERT, feat_width).astype(jnp.bfloat16)


def attend_block(hidden, query_weight, key_weight, value_weight, out_weight):
    snaps, verts, model_width = hidden.shape
    flat = hidden.reshape(snaps * verts, model_width)

    def project(weight):
        return jnp.dot(flat, weight, preferred_element_type=jnp.float32).astype(jnp.bfloat16).reshape(snaps, verts, HEADS, HEAD_DIM)

    query_heads = project(query_weight)
    key_heads = project(key_weight)
    value_heads = project(value_weight)
    scores = jnp.einsum("tvhd,uvhd->vhtu", query_heads.astype(jnp.float32), key_heads.astype(jnp.float32)) * (HEAD_DIM ** -0.5)
    causal = jnp.arange(snaps, dtype=jnp.int32)[:, None] >= jnp.arange(snaps, dtype=jnp.int32)[None, :]
    scores = jnp.where(causal, scores, masked_score)
    row_max = jnp.max(scores, axis=-1, keepdims=True)
    lifted = jnp.exp(scores - row_max)
    weights = (lifted / jnp.sum(lifted, axis=-1, keepdims=True)).astype(jnp.bfloat16)
    context = jnp.einsum("vhtu,uvhd->tvhd", weights.astype(jnp.float32), value_heads.astype(jnp.float32)).astype(jnp.bfloat16)
    context = context.reshape(snaps * verts, model_width)
    result = flat.astype(jnp.float32) + jnp.dot(context, out_weight, preferred_element_type=jnp.float32)
    return result.astype(jnp.bfloat16).reshape(snaps, verts, model_width)


def reference(node_features, tile_rows, tile_cols, tile_counts, tile_values, layer_one, layer_two, query_weight, key_weight, value_weight, out_weight):
    def evolve_snapshot(packed):
        features, tile_block, block_rows, block_cols, slot_count = packed
        spread_one = spread_snapshot(features, tile_block, block_rows, block_cols, slot_count)
        mixed_one = jnp.dot(spread_one, layer_one, preferred_element_type=jnp.float32)
        hidden_one = (features.astype(jnp.float32) + jnp.maximum(mixed_one, 0.0)).astype(jnp.bfloat16)
        spread_two = spread_snapshot(hidden_one, tile_block, block_rows, block_cols, slot_count)
        mixed_two = jnp.dot(spread_two, layer_two, preferred_element_type=jnp.float32)
        return (hidden_one.astype(jnp.float32) + jnp.maximum(mixed_two, 0.0)).astype(jnp.bfloat16)

    hidden_two = lax.map(evolve_snapshot, (node_features, tile_values, tile_rows, tile_cols, tile_counts))
    vert_block = VERT // N_SNAP
    grouped = hidden_two.reshape(SNAPS, N_SNAP, vert_block, D).transpose(1, 0, 2, 3)

    def attend_group(hidden):
        return attend_block(hidden, query_weight, key_weight, value_weight, out_weight)

    attended = lax.map(attend_group, grouped)
    return attended.transpose(1, 0, 2, 3).reshape(SNAPS, VERT, D)
```

```python
import functools
import math

import jax
import jax.numpy as jnp
from jax import lax
from jax.experimental import pallas as pl
from jax.experimental.pallas import tpu as pltpu
from jax.sharding import PartitionSpec as P

HEADS = 8


masked_score = -1e30


def spread_padded(features, tile_block, block_rows, block_cols, slot_count):
    vert_count, feat_width = features.shape
    tile_side = tile_block.shape[1]
    slot_total = tile_block.shape[0]
    block_count = vert_count // tile_side
    blocked = features.reshape(block_count, tile_side, feat_width)
    picked_blocks = blocked[block_cols]
    live_slots = jnp.arange(slot_total, dtype=jnp.int32) < slot_count
    products = jnp.einsum(
        "irc,icf->irf", tile_block, picked_blocks, preferred_element_type=jnp.float32
    )
    products = products * live_slots.astype(jnp.float32)[:, None, None]
    membership = (
        (block_rows[None, :] == jnp.arange(block_count, dtype=jnp.int32)[:, None])
        & live_slots[None, :]
    ).astype(jnp.float32)
    summed = jnp.dot(
        membership,
        products.reshape(slot_total, tile_side * feat_width),
        precision=lax.Precision.HIGHEST,
    )
    return summed.reshape(vert_count, feat_width).astype(jnp.bfloat16)


def attend_local(hidden, query_weight, key_weight, value_weight, out_weight):
    snaps, verts, model_width = hidden.shape
    head_dim = model_width // HEADS
    flat = hidden.reshape(snaps * verts, model_width)

    def project(weight):
        return (
            jnp.dot(flat, weight, preferred_element_type=jnp.float32)
            .astype(jnp.bfloat16)
            .reshape(snaps, verts, HEADS, head_dim)
        )

    query_heads = project(query_weight)
    key_heads = project(key_weight)
    value_heads = project(value_weight)
    scores = jnp.einsum(
        "tvhd,uvhd->vhtu", query_heads, key_heads, preferred_element_type=jnp.float32
    ) * head_dim ** (-0.5)
    causal = (
        jnp.arange(snaps, dtype=jnp.int32)[:, None] >= jnp.arange(snaps, dtype=jnp.int32)[None, :]
    )
    scores = jnp.where(causal, scores, masked_score)
    row_max = jnp.max(scores, axis=-1, keepdims=True)
    lifted = jnp.exp(scores - row_max)
    weights = (lifted / jnp.sum(lifted, axis=-1, keepdims=True)).astype(jnp.bfloat16)
    context = jnp.einsum(
        "vhtu,uvhd->tvhd", weights, value_heads, preferred_element_type=jnp.float32
    ).astype(jnp.bfloat16)
    context = context.reshape(snaps * verts, model_width)
    result = flat.astype(jnp.float32) + jnp.dot(
        context, out_weight, preferred_element_type=jnp.float32
    )
    return result.astype(jnp.bfloat16).reshape(snaps, verts, model_width)


def on_device(
    node_features,
    tile_rows,
    tile_cols,
    tile_counts,
    tile_values,
    layer_one,
    layer_two,
    query_weight,
    key_weight,
    value_weight,
    out_weight,
):
    snap_dev, vert_count, feat_width = node_features.shape
    feat_index = lax.axis_index("feat")

    def spread_all(features):
        spread_pieces = []
        for snapshot in range(snap_dev):
            spread_pieces.append(
                spread_padded(
                    features[snapshot],
                    tile_values[snapshot],
                    tile_rows[snapshot],
                    tile_cols[snapshot],
                    tile_counts[snapshot],
                )
            )
        return jnp.stack(spread_pieces, axis=0)

    def convolve(features, weight):
        spread_rows = spread_all(features).reshape(snap_dev * vert_count, feat_width)
        own_columns = lax.dynamic_slice_in_dim(weight, feat_index * feat_width, feat_width, 1)
        mixed_sum = jnp.dot(
            lax.all_gather(spread_rows, "feat", axis=1, tiled=True),
            own_columns,
            preferred_element_type=jnp.float32,
        )
        mixed_sum = mixed_sum.reshape(snap_dev, vert_count, feat_width)
        return (features.astype(jnp.float32) + jnp.maximum(mixed_sum, 0.0)).astype(jnp.bfloat16)

    hidden_one = convolve(node_features, layer_one)
    hidden_two = convolve(hidden_one, layer_two)
    vertex_rows = lax.all_to_all(
        lax.all_to_all(hidden_two, "snap", split_axis=1, concat_axis=0, tiled=True),
        "feat",
        split_axis=1,
        concat_axis=2,
        tiled=True,
    )
    attended = attend_local(vertex_rows, query_weight, key_weight, value_weight, out_weight)
    return lax.all_to_all(
        lax.all_to_all(attended, "feat", split_axis=2, concat_axis=1, tiled=True),
        "snap",
        split_axis=0,
        concat_axis=1,
        tiled=True,
    )


LANES = 128
SUBLANES = 8
MESH = pl.DeviceIdType.MESH


def fused_kernel(
    n_snap,
    n_feat,
    rows_hbm,
    cols_hbm,
    counts_hbm,
    feat_ref,
    tiles_ref,
    w_one,
    w_two,
    w_query,
    w_key,
    w_value,
    w_out,
    returned,
    tiles,
    weights,
    pieces,
    adjacency,
    features,
    hidden_one,
    hidden_two,
    vertex_rows,
    outgoing,
    load_sem,
    gather_send,
    gather_recv,
    spread_send,
    spread_recv,
    return_send,
    return_recv,
    heard,
    rows_ref,
    cols_ref,
    counts_ref,
):
    snap_dev, feat_width, vert_count = feat_ref.shape
    slot_total, tile_side, _ = tiles.shape
    block_count = vert_count // tile_side
    snaps, vert_dev, width = vertex_rows.shape
    half_snaps = snaps // 2
    parts = n_feat // snap_dev
    part_rows = vert_count // parts
    head_dim = width // HEADS

    me_snap = lax.axis_index("snap")
    me_feat = lax.axis_index("feat")
    part = me_feat % parts
    local = me_feat // parts
    own = me_snap * snap_dev + local
    half = own // half_snaps
    rank = own % half_snaps
    is_low = half == 0
    is_high = half == 1

    def load(source, target, at):
        copy = pltpu.make_async_copy(source, target, load_sem.at[at])
        copy.start()
        return copy

    def settle(ref, semaphore):
        pltpu.make_async_copy(ref, ref, semaphore).wait()

    barrier = pltpu.get_barrier_semaphore()
    plane = 2
    twin = me_snap + 1 - 2 * (me_snap % 2)
    mates = [(me_feat + step) % n_feat for step in range(1, n_feat)]
    has_below = me_snap >= plane
    has_above = me_snap < n_snap - plane
    column_count = has_below.astype(jnp.int32) + has_above.astype(jnp.int32)

    def signal(semaphore, peer):
        pl.semaphore_signal(semaphore, inc=1, device_id=peer, device_id_type=MESH)

    def tell_column(semaphore):
        @pl.when(has_below)
        def _():
            signal(semaphore, (me_snap - plane, me_feat))

        @pl.when(has_above)
        def _():
            signal(semaphore, (me_snap + plane, me_feat))

    def tell_mates(semaphore):
        for mate in mates:
            signal(semaphore, (me_snap, mate))

    tell_mates(barrier)
    signal(barrier, (twin, me_feat))
    tell_column(barrier)
    list_loads = [
        load(ref, kept, 2 + at)
        for at, (ref, kept) in enumerate(
            ((rows_hbm, rows_ref), (cols_hbm, cols_ref), (counts_hbm, counts_ref))
        )
    ]
    tile_load = load(tiles_ref.at[local], tiles, 1)
    pl.semaphore_wait(barrier, n_feat + column_count)

    for step in [n_feat // 2] + [s for s in range(1, n_feat) if s != n_feat // 2]:
        peer = (me_feat + step) % n_feat
        pltpu.make_async_remote_copy(
            src_ref=feat_ref.at[peer // parts],
            dst_ref=pieces.at[me_feat],
            send_sem=gather_send,
            recv_sem=gather_recv,
            device_id=(me_snap, peer),
            device_id_type=MESH,
        ).start()
    for at, ref in enumerate((w_one, w_two, w_query, w_key, w_value, w_out)):
        load(ref, weights.at[at], 5)
    own_load = load(feat_ref.at[local], pieces.at[me_feat], 0)

    hops = n_snap // plane - 2
    for hop in range(hops):
        tell_column(heard.at[hop])
        if hop + 1 < hops:
            pl.semaphore_wait(heard.at[hop], column_count)

    tile_load.wait()
    for copy in list_loads:
        copy.wait()
    slot_count = counts_ref[local]
    strip = 2 * SUBLANES
    places = []
    for slot in range(slot_total):
        place = rows_ref[local, slot] * block_count + cols_ref[local, slot]
        place = jnp.where(slot < slot_count, place, -1)
        places.append(jnp.full((strip, tile_side), place, jnp.int32))

    def build(at, carry):
        first = pl.multiple_of(at * strip, strip)
        listed = [
            tiles[slot, pl.ds(first, strip), :].astype(jnp.float32) for slot in range(slot_total)
        ]
        for row in range(block_count):
            for col in range(block_count):
                summed = jnp.zeros((strip, tile_side), jnp.float32)
                for slot in range(slot_total):
                    summed += jnp.where(
                        places[slot] == row * block_count + col, listed[slot], 0.0
                    )
                start = pl.multiple_of(row * tile_side + first, strip)
                adjacency[pl.ds(start, strip), col * tile_side : (col + 1) * tile_side] = (
                    summed.astype(jnp.bfloat16)
                )
        return carry

    strips = tile_side // strip
    lax.fori_loop(0, strips // 2, build, 0)
    pl.semaphore_wait(heard.at[hops - 1], column_count)
    signal(heard.at[hops], (twin, me_feat))
    lax.fori_loop(strips // 2, strips, build, 0)
    pl.semaphore_wait(heard.at[hops], 1)
    tell_mates(heard.at[hops + 1])

    settle(weights, load_sem.at[5])
    settle(pieces.at[pl.ds(0, n_feat - 1)], gather_recv)
    own_load.wait()
    features[...] = jnp.transpose(pieces[...].reshape(width, vert_count))

    def mix(lhs, source, before, weight):
        spread = jnp.dot(lhs, source, preferred_element_type=jnp.float32)
        mixed = jnp.dot(
            spread.astype(jnp.bfloat16), weight, preferred_element_type=jnp.float32
        )
        return (before.astype(jnp.float32) + jnp.maximum(mixed, 0.0)).astype(jnp.bfloat16)

    hidden_one[...] = mix(adjacency[...], features[...], features[...], weights[0])
    pl.semaphore_wait(heard.at[hops + 1], len(mates))

    def spread_to(target_half, peer):
        target = target_half * half_snaps + peer
        pltpu.make_async_remote_copy(
            src_ref=hidden_two.at[peer],
            dst_ref=vertex_rows.at[own],
            send_sem=spread_send.at[target_half],
            recv_sem=spread_recv.at[half],
            device_id=(target // snap_dev, (target % snap_dev) * parts + part),
            device_id_type=MESH,
        ).start()

    def spread_half(target_half):
        for step in [half_snaps // 2] + [
            s for s in range(1, half_snaps) if s != half_snaps // 2
        ]:
            spread_to(target_half, (rank + step) % half_snaps)

    own_rows = pl.ds(pl.multiple_of(part * part_rows, part_rows), part_rows)
    hidden_two[...] = mix(
        adjacency[own_rows, :], hidden_one[...], hidden_one[own_rows, :], weights[1]
    ).reshape(half_snaps, vert_dev, width)
    side = half_snaps // 2
    far = [side + (rank + step) % side for step in range(side)]
    near = [(rank + step) % side for step in range(side)]

    @pl.when(is_low)
    def _():
        spread_half(0)
        for peer in far + near:
            spread_to(1, peer)

    @pl.when(is_high)
    def _():
        spread_half(1)

    vertex_rows[own] = hidden_two[rank]

    groups = vert_dev // SUBLANES
    group_rows = half_snaps * SUBLANES
    columns = HEADS * group_rows

    def split(array):
        array = array.reshape(half_snaps, groups, SUBLANES, width)
        return [array[:, at].reshape(group_rows, width) for at in range(groups)]

    def project(flat, at):
        return split(jnp.dot(flat, weights[at], preferred_element_type=jnp.float32))

    def score(keys, queries):
        return lax.dot_general(
            keys.astype(jnp.bfloat16),
            queries,
            (((1,), (1,)), ((), ())),
            preferred_element_type=jnp.float32,
        )

    row_at = lax.broadcasted_iota(jnp.int32, (group_rows, columns), 0)
    col_at = lax.broadcasted_iota(jnp.int32, (group_rows, columns), 1) % group_rows
    same = row_at % SUBLANES == col_at % SUBLANES
    visible = same & (row_at // SUBLANES <= col_at // SUBLANES)
    visible_low = same & (jnp.full((group_rows, columns), half, jnp.int32) == 1)
    lane_head = lax.broadcasted_iota(jnp.int32, (group_rows, width), 1) // head_dim
    factor = head_dim ** (-0.5) * math.log2(math.e)

    settle(vertex_rows.at[pl.ds(0, half_snaps - 1)], spread_recv.at[half])
    own_rows = vertex_rows[pl.ds(half * half_snaps, half_snaps)]
    flat = own_rows.reshape(half_snaps * vert_dev, width)
    before = split(flat.astype(jnp.float32))
    queries = [
        jnp.concatenate(
            [
                jnp.where(lane_head == head, query, 0.0).astype(jnp.bfloat16)
                for head in range(HEADS)
            ],
            axis=0,
        )
        for query in project(flat, 2)
    ]
    keys, values = project(flat, 3), project(flat, 4)
    scores = [
        jnp.where(visible, score(keys[at], queries[at]), masked_score)
        for at in range(groups)
    ]

    @pl.when(is_high)
    def _():
        settle(vertex_rows.at[pl.ds(0, half_snaps)], spread_recv.at[0])

    flat_low = vertex_rows[pl.ds(0, half_snaps)].reshape(half_snaps * vert_dev, width)
    keys_low, values_low = project(flat_low, 3), project(flat_low, 4)
    pair = 2 * group_rows
    pair_dims = 2 * head_dim
    pair_row = lax.broadcasted_iota(jnp.int32, (pair_dims, pair), 0) // head_dim
    pair_col = lax.broadcasted_iota(jnp.int32, (pair_dims, pair), 1) // group_rows
    contexts = []
    for at in range(groups):
        score_low = jnp.where(visible_low, score(keys_low[at], queries[at]), masked_score)
        score_own = scores[at]
        highest = jnp.maximum(
            jnp.max(score_low, axis=0, keepdims=True), jnp.max(score_own, axis=0, keepdims=True)
        )
        lifted_low = jnp.exp2((score_low - highest) * factor)
        lifted_own = jnp.exp2((score_own - highest) * factor)
        scale = 1.0 / (
            jnp.sum(lifted_low, axis=0, keepdims=True) + jnp.sum(lifted_own, axis=0, keepdims=True)
        )
        shares = jnp.concatenate(
            [(lifted_low * scale).astype(jnp.bfloat16), (lifted_own * scale).astype(jnp.bfloat16)],
            axis=0,
        )
        value = jnp.transpose(
            jnp.concatenate([values_low[at], values[at]], axis=0).astype(jnp.bfloat16)
        )
        context = []
        for at_pair in range(HEADS // 2):
            product = jnp.dot(
                value[at_pair * pair_dims : (at_pair + 1) * pair_dims],
                shares[:, at_pair * pair : (at_pair + 1) * pair],
                preferred_element_type=jnp.float32,
            )
            context.append(jnp.where(pair_row == pair_col, product, 0.0).astype(jnp.bfloat16))
        contexts.append(jnp.transpose(jnp.concatenate(context, axis=0)))
    mixed = jnp.dot(
        jnp.concatenate(contexts, axis=0), weights[5], preferred_element_type=jnp.float32
    ).reshape(groups, 2, group_rows, width)
    results = [
        (before[at] + (mixed[at, 0] + mixed[at, 1])).reshape(half_snaps, 1, SUBLANES, width)
        for at in range(groups)
    ]
    half_dev = n_snap // 2
    evolved = jnp.concatenate(results, axis=1).reshape(half_dev, snap_dev, vert_dev, width)

    low = lax.broadcasted_iota(jnp.int32, (half_dev * vert_dev, LANES), 1) < feat_width
    for at in range(0, n_feat, 2):
        lanes = slice(at * feat_width, (at + 2) * feat_width)
        first = evolved[:, 0, :, lanes].reshape(half_dev * vert_dev, LANES)
        second = evolved[:, 1, :, lanes].reshape(half_dev * vert_dev, LANES)
        even = jnp.where(low, first, pltpu.roll(second, feat_width, 1))
        odd = jnp.where(low, pltpu.roll(first, feat_width, 1), second)
        outgoing[at] = even.astype(jnp.bfloat16).reshape(half_dev, vert_dev, LANES)
        outgoing[at + 1] = odd.astype(jnp.bfloat16).reshape(half_dev, vert_dev, LANES)

    total = half_dev * n_feat
    me = (me_snap % half_dev) * n_feat + me_feat
    for step in sorted(range(1, total), key=lambda s: abs(2 * s - total)):
        peer = (me + step) % total
        pltpu.make_async_remote_copy(
            src_ref=outgoing.at[peer % n_feat, peer // n_feat],
            dst_ref=returned.at[part, rank],
            send_sem=return_send,
            recv_sem=return_recv,
            device_id=(half * half_dev + peer // n_feat, peer % n_feat),
            device_id_type=MESH,
        ).start()
    own_copy = load(outgoing.at[me_feat, me_snap % half_dev], returned.at[part, rank], 0)
    settle(pieces.at[pl.ds(0, n_feat - 1)], gather_send)

    @pl.when(is_low)
    def _():
        settle(hidden_two.at[pl.ds(0, half_snaps)], spread_send.at[1])
        settle(hidden_two.at[pl.ds(0, half_snaps - 1)], spread_send.at[0])

    @pl.when(is_high)
    def _():
        settle(hidden_two.at[pl.ds(0, half_snaps - 1)], spread_send.at[1])

    own_copy.wait()
    everyone = outgoing.reshape(total, vert_dev, LANES).at[pl.ds(0, total - 1)]
    settle(everyone, return_recv)
    settle(everyone, return_send)


def on_device_fused(n_snap, n_feat, *operands):
    node_features, _, _, _, tile_values, layer_one = operands[:6]
    snap_dev, vert_count, feat_width = node_features.shape
    _, slot_total, tile_side, _ = tile_values.shape
    width = layer_one.shape[0]
    parts = n_feat // snap_dev
    snaps = n_snap * snap_dev
    half_snaps = snaps // 2
    vert_dev = vert_count // (parts * half_snaps)
    kept = jnp.bfloat16
    result = pl.pallas_call(
        functools.partial(fused_kernel, n_snap, n_feat),
        out_shape=pltpu.VMEM((parts, half_snaps, vert_dev, LANES), kept),
        in_specs=[pl.BlockSpec(memory_space=pltpu.HBM)] * 11,
        out_specs=pl.BlockSpec(memory_space=pltpu.VMEM),
        scratch_shapes=[
            pltpu.VMEM((slot_total, tile_side, tile_side), kept),
            pltpu.VMEM((6, width, width), kept),
            pltpu.VMEM((n_feat, feat_width, vert_count), kept),
            pltpu.VMEM((vert_count, vert_count), kept),
            pltpu.VMEM((vert_count, width), kept),
            pltpu.VMEM((vert_count, width), kept),
            pltpu.VMEM((half_snaps, vert_dev, width), kept),
            pltpu.VMEM((snaps, vert_dev, width), kept),
            pltpu.VMEM((n_feat, n_snap // 2, vert_dev, LANES), kept),
            pltpu.SemaphoreType.DMA((6,)),
            pltpu.SemaphoreType.DMA,
            pltpu.SemaphoreType.DMA,
            pltpu.SemaphoreType.DMA((2,)),
            pltpu.SemaphoreType.DMA((2,)),
            pltpu.SemaphoreType.DMA,
            pltpu.SemaphoreType.DMA,
            pltpu.SemaphoreType.REGULAR((n_snap // 2,)),
            pltpu.SMEM((snap_dev, slot_total), jnp.int32),
            pltpu.SMEM((snap_dev, slot_total), jnp.int32),
            pltpu.SMEM((snap_dev,), jnp.int32),
        ],
        compiler_params=pltpu.CompilerParams(collective_id=0, has_side_effects=True),
    )(*operands[1:4], node_features.transpose(0, 2, 1), *operands[4:])
    result = jnp.transpose(result.reshape(vert_count, LANES))
    return result.reshape(snap_dev, feat_width, vert_count).transpose(0, 2, 1)


def dispatch(n_snap, n_feat, *operands):
    snap_dev, vert_count, feat_width = operands[0].shape
    slot_total = operands[4].shape[1]
    snaps = n_snap * snap_dev
    fits = (
        snap_dev == 2
        and 2 * feat_width == LANES
        and n_feat % snap_dev == 0
        and n_feat % 2 == 0
        and n_snap >= 8
        and n_snap % 4 == 0
        and vert_count % (n_feat // snap_dev * snaps * SUBLANES) == 0
        and snaps * SUBLANES == LANES
        and slot_total <= 16
        and vert_count <= 1024
    )
    if fits:
        return on_device_fused(n_snap, n_feat, *operands)
    return on_device(*operands)


def solution(mesh):
    placed = (
        P("snap", None, "feat"),
        P("snap", None),
        P("snap", None),
        P("snap"),
        P("snap", None, None, None),
        P(),
        P(),
        P(),
        P(),
        P(),
        P(),
    )
    return jax.shard_map(
        functools.partial(dispatch, mesh.shape["snap"], mesh.shape["feat"]), mesh=mesh, in_specs=placed, out_specs=P("snap", None, "feat"), check_vma=False
    )
```

```python
import functools
import math

import jax
import jax.numpy as jnp
from jax import lax
from jax.experimental import pallas as pl
from jax.experimental.pallas import tpu as pltpu
from jax.sharding import PartitionSpec as P

HEADS = 8


masked_score = -1e30


def spread_padded(features, tile_block, block_rows, block_cols, slot_count):
    vert_count, feat_width = features.shape
    tile_side = tile_block.shape[1]
    slot_total = tile_block.shape[0]
    block_count = vert_count // tile_side
    blocked = features.reshape(block_count, tile_side, feat_width)
    picked_blocks = blocked[block_cols]
    live_slots = jnp.arange(slot_total, dtype=jnp.int32) < slot_count
    products = jnp.einsum(
        "irc,icf->irf", tile_block, picked_blocks, preferred_element_type=jnp.float32
    )
    products = products * live_slots.astype(jnp.float32)[:, None, None]
    membership = (
        (block_rows[None, :] == jnp.arange(block_count, dtype=jnp.int32)[:, None])
        & live_slots[None, :]
    ).astype(jnp.float32)
    summed = jnp.dot(
        membership,
        products.reshape(slot_total, tile_side * feat_width),
        precision=lax.Precision.HIGHEST,
    )
    return summed.reshape(vert_count, feat_width).astype(jnp.bfloat16)


def attend_local(hidden, query_weight, key_weight, value_weight, out_weight):
    snaps, verts, model_width = hidden.shape
    head_dim = model_width // HEADS
    flat = hidden.reshape(snaps * verts, model_width)

    def project(weight):
        return (
            jnp.dot(flat, weight, preferred_element_type=jnp.float32)
            .astype(jnp.bfloat16)
            .reshape(snaps, verts, HEADS, head_dim)
        )

    query_heads = project(query_weight)
    key_heads = project(key_weight)
    value_heads = project(value_weight)
    scores = jnp.einsum(
        "tvhd,uvhd->vhtu", query_heads, key_heads, preferred_element_type=jnp.float32
    ) * head_dim ** (-0.5)
    causal = (
        jnp.arange(snaps, dtype=jnp.int32)[:, None] >= jnp.arange(snaps, dtype=jnp.int32)[None, :]
    )
    scores = jnp.where(causal, scores, masked_score)
    row_max = jnp.max(scores, axis=-1, keepdims=True)
    lifted = jnp.exp(scores - row_max)
    weights = (lifted / jnp.sum(lifted, axis=-1, keepdims=True)).astype(jnp.bfloat16)
    context = jnp.einsum(
        "vhtu,uvhd->tvhd", weights, value_heads, preferred_element_type=jnp.float32
    ).astype(jnp.bfloat16)
    context = context.reshape(snaps * verts, model_width)
    result = flat.astype(jnp.float32) + jnp.dot(
        context, out_weight, preferred_element_type=jnp.float32
    )
    return result.astype(jnp.bfloat16).reshape(snaps, verts, model_width)


def on_device(
    node_features,
    tile_rows,
    tile_cols,
    tile_counts,
    tile_values,
    layer_one,
    layer_two,
    query_weight,
    key_weight,
    value_weight,
    out_weight,
):
    snap_dev, vert_count, feat_width = node_features.shape
    feat_index = lax.axis_index("feat")

    def spread_all(features):
        spread_pieces = []
        for snapshot in range(snap_dev):
            spread_pieces.append(
                spread_padded(
                    features[snapshot],
                    tile_values[snapshot],
                    tile_rows[snapshot],
                    tile_cols[snapshot],
                    tile_counts[snapshot],
                )
            )
        return jnp.stack(spread_pieces, axis=0)

    def convolve(features, weight):
        spread_rows = spread_all(features).reshape(snap_dev * vert_count, feat_width)
        own_columns = lax.dynamic_slice_in_dim(weight, feat_index * feat_width, feat_width, 1)
        mixed_sum = jnp.dot(
            lax.all_gather(spread_rows, "feat", axis=1, tiled=True),
            own_columns,
            preferred_element_type=jnp.float32,
        )
        mixed_sum = mixed_sum.reshape(snap_dev, vert_count, feat_width)
        return (features.astype(jnp.float32) + jnp.maximum(mixed_sum, 0.0)).astype(jnp.bfloat16)

    hidden_one = convolve(node_features, layer_one)
    hidden_two = convolve(hidden_one, layer_two)
    vertex_rows = lax.all_to_all(
        lax.all_to_all(hidden_two, "snap", split_axis=1, concat_axis=0, tiled=True),
        "feat",
        split_axis=1,
        concat_axis=2,
        tiled=True,
    )
    attended = attend_local(vertex_rows, query_weight, key_weight, value_weight, out_weight)
    return lax.all_to_all(
        lax.all_to_all(attended, "feat", split_axis=2, concat_axis=1, tiled=True),
        "snap",
        split_axis=0,
        concat_axis=1,
        tiled=True,
    )


LANES = 128
CHUNKS = 4
SUBLANES = 8
MESH = pl.DeviceIdType.MESH


def fused_kernel(
    n_snap,
    n_feat,
    rows_hbm,
    cols_hbm,
    counts_hbm,
    feat_ref,
    tiles_ref,
    w_one,
    w_two,
    w_query,
    w_key,
    w_value,
    w_out,
    returned,
    tiles,
    weights,
    pieces,
    adjacency,
    features,
    hidden_one,
    hidden_two,
    vertex_rows,
    outgoing,
    load_sem,
    gather_send,
    gather_recv,
    spread_send,
    spread_recv,
    return_send,
    return_recv,
    heard,
    rows_ref,
    cols_ref,
    counts_ref,
):
    snap_dev, feat_width, vert_count = feat_ref.shape
    slot_total, tile_side, _ = tiles.shape
    block_count = vert_count // tile_side
    snaps, vert_dev, width = vertex_rows.shape
    half_snaps = snaps // 2
    parts = n_feat // snap_dev
    part_rows = vert_count // parts
    head_dim = width // HEADS

    me_snap = lax.axis_index("snap")
    me_feat = lax.axis_index("feat")
    part = me_feat % parts
    local = me_feat // parts
    own = me_snap * snap_dev + local
    half = own // half_snaps
    rank = own % half_snaps
    is_low = half == 0
    is_high = half == 1

    def load(source, target, at):
        copy = pltpu.make_async_copy(source, target, load_sem.at[at])
        copy.start()
        return copy

    def settle(ref, semaphore):
        pltpu.make_async_copy(ref, ref, semaphore).wait()

    barrier = pltpu.get_barrier_semaphore()
    plane = 2
    twin = me_snap + 1 - 2 * (me_snap % 2)
    mates = [(me_feat + step) % n_feat for step in range(1, n_feat)]
    has_below = me_snap >= plane
    has_above = me_snap < n_snap - plane
    column_count = has_below.astype(jnp.int32) + has_above.astype(jnp.int32)

    def signal(semaphore, peer):
        pl.semaphore_signal(semaphore, inc=1, device_id=peer, device_id_type=MESH)

    def tell_column(semaphore):
        @pl.when(has_below)
        def _():
            signal(semaphore, (me_snap - plane, me_feat))

        @pl.when(has_above)
        def _():
            signal(semaphore, (me_snap + plane, me_feat))

    def tell_mates(semaphore):
        for mate in mates:
            signal(semaphore, (me_snap, mate))

    tell_mates(barrier)
    signal(barrier, (twin, me_feat))
    tell_column(barrier)
    list_loads = [
        load(ref, kept, 2 + at)
        for at, (ref, kept) in enumerate(
            ((rows_hbm, rows_ref), (cols_hbm, cols_ref), (counts_hbm, counts_ref))
        )
    ]
    tile_load = load(tiles_ref.at[local], tiles, 1)
    pl.semaphore_wait(barrier, n_feat + column_count)

    partner = (me_feat + parts) % n_feat
    mate = local * parts + 1 - part
    chunk = feat_width // CHUNKS
    spans = [pl.ds(at * chunk, chunk) for at in range(CHUNKS)]
    for at in range(CHUNKS):
        pltpu.make_async_remote_copy(
            src_ref=feat_ref.at[partner // parts, spans[at]],
            dst_ref=pieces.at[me_feat, spans[at]],
            send_sem=gather_send,
            recv_sem=gather_recv.at[at],
            device_id=(me_snap, partner),
            device_id_type=MESH,
        ).start()
    pltpu.make_async_remote_copy(
        src_ref=feat_ref.at[local],
        dst_ref=pieces.at[me_feat],
        send_sem=gather_send,
        recv_sem=gather_recv.at[CHUNKS],
        device_id=(me_snap, mate),
        device_id_type=MESH,
    ).start()

    def relay(at):
        passed = pieces.at[partner, spans[at]]
        settle(passed, gather_recv.at[at])
        pltpu.make_async_remote_copy(
            src_ref=passed,
            dst_ref=passed,
            send_sem=gather_send,
            recv_sem=gather_recv.at[CHUNKS],
            device_id=(me_snap, mate),
            device_id_type=MESH,
        ).start()

    for at, ref in enumerate((w_one, w_two, w_query, w_key, w_value, w_out)):
        load(ref, weights.at[at], 5)
    own_load = load(feat_ref.at[local], pieces.at[me_feat], 0)

    hops = n_snap // plane - 2
    tell_column(heard.at[0])
    tile_load.wait()
    for copy in list_loads:
        copy.wait()
    slot_count = counts_ref[local]
    strip = 2 * SUBLANES
    places = []
    for slot in range(slot_total):
        place = rows_ref[local, slot] * block_count + cols_ref[local, slot]
        place = jnp.where(slot < slot_count, place, -1)
        places.append(jnp.full((strip, tile_side), place, jnp.int32))

    def build(at, carry):
        first = pl.multiple_of(at * strip, strip)
        listed = [
            tiles[slot, pl.ds(first, strip), :].astype(jnp.float32) for slot in range(slot_total)
        ]
        for row in range(block_count):
            for col in range(block_count):
                summed = jnp.zeros((strip, tile_side), jnp.float32)
                for slot in range(slot_total):
                    summed += jnp.where(
                        places[slot] == row * block_count + col, listed[slot], 0.0
                    )
                start = pl.multiple_of(row * tile_side + first, strip)
                adjacency[pl.ds(start, strip), col * tile_side : (col + 1) * tile_side] = (
                    summed.astype(jnp.bfloat16)
                )
        return carry

    strips = tile_side // strip
    lax.fori_loop(0, strips // 2, build, 0)
    for hop in range(hops - 1):
        pl.semaphore_wait(heard.at[hop], column_count)
        tell_column(heard.at[hop + 1])
    lax.fori_loop(strips // 2, strips, build, 0)
    pl.semaphore_wait(heard.at[hops - 1], column_count)
    signal(heard.at[hops], (twin, me_feat))
    for at in range(CHUNKS):
        relay(at)
    pl.semaphore_wait(heard.at[hops], 1)
    tell_mates(heard.at[hops + 1])

    settle(weights, load_sem.at[5])
    settle(pieces.at[pl.ds(0, n_feat // 2)], gather_recv.at[CHUNKS])
    own_load.wait()
    features[...] = jnp.transpose(pieces[...].reshape(width, vert_count))

    def mix(lhs, source, before, weight):
        spread = jnp.dot(lhs, source, preferred_element_type=jnp.float32)
        mixed = jnp.dot(
            spread.astype(jnp.bfloat16), weight, preferred_element_type=jnp.float32
        )
        return (before.astype(jnp.float32) + jnp.maximum(mixed, 0.0)).astype(jnp.bfloat16)

    hidden_one[...] = mix(adjacency[...], features[...], features[...], weights[0])
    pl.semaphore_wait(heard.at[hops + 1], len(mates))

    def spread_to(target_half, peer):
        target = target_half * half_snaps + peer
        pltpu.make_async_remote_copy(
            src_ref=hidden_two.at[peer],
            dst_ref=vertex_rows.at[own],
            send_sem=spread_send.at[target_half],
            recv_sem=spread_recv.at[half],
            device_id=(target // snap_dev, (target % snap_dev) * parts + part),
            device_id_type=MESH,
        ).start()

    def flip(index, mask):
        flipped = 0
        for bit in (4, 2, 1):
            digit = index // bit % 2
            flipped = flipped + bit * (1 - digit if mask & bit else digit)
        return flipped

    def spread_half(target_half):
        for mask in (7, 6, 5, 3, 4, 2, 1):
            spread_to(target_half, flip(rank, mask))

    near = rank % (half_snaps // 2)
    own_rows = pl.ds(pl.multiple_of(part * part_rows, part_rows), part_rows)
    hidden_two[...] = mix(
        adjacency[own_rows, :], hidden_one[...], hidden_one[own_rows, :], weights[1]
    ).reshape(half_snaps, vert_dev, width)

    @pl.when(is_low)
    def _():
        spread_half(0)
        for high in (1, 0):
            for mask in (3, 2, 1, 0):
                spread_to(1, high * (half_snaps // 2) + flip(near, mask))
    @pl.when(is_high)
    def _():
        spread_half(1)

    vertex_rows[own] = hidden_two[rank]

    groups = vert_dev // SUBLANES
    group_rows = half_snaps * SUBLANES
    pair = 2 * group_rows
    pair_dims = 2 * head_dim
    quads = width // LANES
    quad_pairs = LANES // pair_dims
    half_dev = n_snap // 2

    def split(array):
        array = array.reshape(half_snaps, groups, SUBLANES, width)
        return [array[:, at].reshape(group_rows, width) for at in range(groups)]

    def project(flat, at):
        return split(jnp.dot(flat, weights[at], preferred_element_type=jnp.float32))

    def score(keys, turned):
        keys = keys.astype(jnp.bfloat16)
        return [
            jnp.dot(
                keys[:, at * LANES : (at + 1) * LANES],
                turned[at],
                preferred_element_type=jnp.float32,
            )
            for at in range(quads)
        ]

    quad_columns = quad_pairs * pair
    row_at = lax.broadcasted_iota(jnp.int32, (group_rows, quad_columns), 0)
    col_at = lax.broadcasted_iota(jnp.int32, (group_rows, quad_columns), 1) % group_rows
    same = row_at % SUBLANES == col_at % SUBLANES
    visible = same & (row_at // SUBLANES <= col_at // SUBLANES)
    factor = head_dim ** (-0.5) * math.log2(math.e)
    none = jnp.zeros((pair_dims, pair), jnp.bfloat16)
    ones = jnp.ones((2 * SUBLANES, group_rows), jnp.bfloat16)

    settle(vertex_rows.at[pl.ds(0, half_snaps - 1)], spread_recv.at[half])
    own_rows = vertex_rows[pl.ds(half * half_snaps, half_snaps)]
    flat = own_rows.reshape(half_snaps * vert_dev, width)
    doubled = jnp.concatenate(
        [query for query in project(flat, 2) for _ in range(2)], axis=0
    )
    turned = jnp.transpose(doubled.astype(jnp.bfloat16))
    turned_head = lax.broadcasted_iota(jnp.int32, turned.shape, 0) // head_dim
    turned_side = lax.broadcasted_iota(jnp.int32, turned.shape, 1) // group_rows
    turned = jnp.where(turned_head % 2 == turned_side % 2, turned, 0.0)
    queries = []
    for at in range(groups):
        columns = turned[:, at * pair : (at + 1) * pair]
        queries.append(
            [
                jnp.concatenate(
                    [
                        jnp.concatenate(
                            [
                                columns[
                                    (quad * quad_pairs + inner) * pair_dims : (
                                        quad * quad_pairs + inner + 1
                                    )
                                    * pair_dims
                                ]
                                if inner == outer
                                else none
                                for inner in range(quad_pairs)
                            ],
                            axis=0,
                        )
                        for outer in range(quad_pairs)
                    ],
                    axis=1,
                )
                for quad in range(quads)
            ]
        )
    keys, values = project(flat, 3), project(flat, 4)
    scores = [
        [jnp.where(visible, each, masked_score) for each in score(keys[at], queries[at])]
        for at in range(groups)
    ]

    def attend(scores_of, values_of):
        lane_odd = lax.broadcasted_iota(jnp.int32, (group_rows, width), 1) // head_dim % 2 == 1
        contexts = []
        for at in range(groups):
            value = jnp.transpose(
                jnp.concatenate([each[at] for each in values_of], axis=0).astype(jnp.bfloat16)
            )
            tail = jnp.concatenate([ones] * len(values_of), axis=1)
            context = []
            for quad in range(quads):
                listed = [each[at][quad] for each in scores_of]
                highest = functools.reduce(
                    jnp.maximum, [jnp.max(each, axis=0, keepdims=True) for each in listed]
                )
                shares = jnp.concatenate(
                    [
                        jnp.exp2((each - highest) * factor).astype(jnp.bfloat16)
                        for each in listed
                    ],
                    axis=0,
                )
                for inner in range(quad_pairs):
                    first = (quad * quad_pairs + inner) * pair_dims
                    product = jnp.dot(
                        jnp.concatenate([value[first : first + pair_dims], tail], axis=0),
                        shares[:, inner * pair : (inner + 1) * pair],
                        preferred_element_type=jnp.float32,
                    )
                    scale = 1.0 / product[pair_dims : pair_dims + 1]
                    context.append((product[:pair_dims] * scale).astype(jnp.bfloat16))
            context = jnp.transpose(jnp.concatenate(context, axis=0))
            contexts.append(jnp.where(lane_odd, context[group_rows:], context[:group_rows]))
        mixed = jnp.dot(
            jnp.concatenate(contexts, axis=0), weights[5], preferred_element_type=jnp.float32
        ).reshape(groups, half_snaps, SUBLANES, width)
        before = own_rows.astype(jnp.float32).reshape(half_snaps, groups, SUBLANES, width)
        evolved = jnp.concatenate(
            [
                before[:, at : at + 1] + mixed[at].reshape(half_snaps, 1, SUBLANES, width)
                for at in range(groups)
            ],
            axis=1,
        ).reshape(half_dev, snap_dev, vert_dev, width)
        low = lax.broadcasted_iota(jnp.int32, (half_dev * vert_dev, LANES), 1) < feat_width
        for at in range(0, n_feat, 2):
            lanes = slice(at * feat_width, (at + 2) * feat_width)
            first = evolved[:, 0, :, lanes].reshape(half_dev * vert_dev, LANES)
            second = evolved[:, 1, :, lanes].reshape(half_dev * vert_dev, LANES)
            even = jnp.where(low, first, pltpu.roll(second, feat_width, 1))
            odd = jnp.where(low, pltpu.roll(first, feat_width, 1), second)
            outgoing[at] = even.astype(jnp.bfloat16).reshape(half_dev, vert_dev, LANES)
            outgoing[at + 1] = odd.astype(jnp.bfloat16).reshape(half_dev, vert_dev, LANES)

    @pl.when(is_low)
    def _():
        attend([scores], [values])

    @pl.when(is_high)
    def _():
        settle(vertex_rows.at[pl.ds(0, half_snaps)], spread_recv.at[0])
        flat_low = vertex_rows[pl.ds(0, half_snaps)].reshape(half_snaps * vert_dev, width)
        keys_low, values_low = project(flat_low, 3), project(flat_low, 4)
        scores_low = [
            [jnp.where(same, each, masked_score) for each in score(keys_low[at], queries[at])]
            for at in range(groups)
        ]
        attend([scores_low, scores], [values_low, values])

    total = half_dev * n_feat
    me = (me_snap % half_dev) * n_feat + me_feat
    for mask in (14, 15, 12, 13, 10, 11, 6, 7, 8, 9, 4, 5, 2, 3, 1):
        peer = flip(me // 2, mask // 2) * 2 + (1 - me % 2 if mask % 2 else me % 2)
        pltpu.make_async_remote_copy(
            src_ref=outgoing.at[peer % n_feat, peer // n_feat],
            dst_ref=returned.at[part, rank],
            send_sem=return_send,
            recv_sem=return_recv,
            device_id=(half * half_dev + peer // n_feat, peer % n_feat),
            device_id_type=MESH,
        ).start()
    own_copy = load(outgoing.at[me_feat, me_snap % half_dev], returned.at[part, rank], 0)
    settle(pieces.at[pl.ds(0, n_feat - 1)], gather_send)

    @pl.when(is_low)
    def _():
        settle(hidden_two.at[pl.ds(0, half_snaps)], spread_send.at[1])
        settle(hidden_two.at[pl.ds(0, half_snaps - 1)], spread_send.at[0])

    @pl.when(is_high)
    def _():
        settle(hidden_two.at[pl.ds(0, half_snaps - 1)], spread_send.at[1])

    own_copy.wait()
    everyone = outgoing.reshape(total, vert_dev, LANES).at[pl.ds(0, total - 1)]
    settle(everyone, return_recv)
    settle(everyone, return_send)


def on_device_fused(n_snap, n_feat, *operands):
    node_features, _, _, _, tile_values, layer_one = operands[:6]
    snap_dev, vert_count, feat_width = node_features.shape
    _, slot_total, tile_side, _ = tile_values.shape
    width = layer_one.shape[0]
    parts = n_feat // snap_dev
    snaps = n_snap * snap_dev
    half_snaps = snaps // 2
    vert_dev = vert_count // (parts * half_snaps)
    kept = jnp.bfloat16
    result = pl.pallas_call(
        functools.partial(fused_kernel, n_snap, n_feat),
        out_shape=pltpu.VMEM((parts, half_snaps, vert_dev, LANES), kept),
        in_specs=[pl.BlockSpec(memory_space=pltpu.HBM)] * 11,
        out_specs=pl.BlockSpec(memory_space=pltpu.VMEM),
        scratch_shapes=[
            pltpu.VMEM((slot_total, tile_side, tile_side), kept),
            pltpu.VMEM((6, width, width), kept),
            pltpu.VMEM((n_feat, feat_width, vert_count), kept),
            pltpu.VMEM((vert_count, vert_count), kept),
            pltpu.VMEM((vert_count, width), kept),
            pltpu.VMEM((vert_count, width), kept),
            pltpu.VMEM((half_snaps, vert_dev, width), kept),
            pltpu.VMEM((snaps, vert_dev, width), kept),
            pltpu.VMEM((n_feat, n_snap // 2, vert_dev, LANES), kept),
            pltpu.SemaphoreType.DMA((6,)),
            pltpu.SemaphoreType.DMA,
            pltpu.SemaphoreType.DMA((CHUNKS + 1,)),
            pltpu.SemaphoreType.DMA((2,)),
            pltpu.SemaphoreType.DMA((2,)),
            pltpu.SemaphoreType.DMA,
            pltpu.SemaphoreType.DMA,
            pltpu.SemaphoreType.REGULAR((n_snap // 2,)),
            pltpu.SMEM((snap_dev, slot_total), jnp.int32),
            pltpu.SMEM((snap_dev, slot_total), jnp.int32),
            pltpu.SMEM((snap_dev,), jnp.int32),
        ],
        compiler_params=pltpu.CompilerParams(collective_id=0, has_side_effects=True),
    )(*operands[1:4], node_features.transpose(0, 2, 1), *operands[4:])
    result = jnp.transpose(result.reshape(vert_count, LANES))
    return result.reshape(snap_dev, feat_width, vert_count).transpose(0, 2, 1)


def dispatch(n_snap, n_feat, *operands):
    snap_dev, vert_count, feat_width = operands[0].shape
    slot_total = operands[4].shape[1]
    snaps = n_snap * snap_dev
    fits = (
        snap_dev == 2
        and 2 * feat_width == LANES
        and n_feat == 2 * snap_dev
        and n_snap >= 8
        and n_snap % 4 == 0
        and vert_count % (n_feat // snap_dev * snaps * SUBLANES) == 0
        and snaps * SUBLANES == LANES
        and slot_total <= 16
        and vert_count <= 1024
    )
    if fits:
        return on_device_fused(n_snap, n_feat, *operands)
    return on_device(*operands)


def solution(mesh):
    placed = (
        P("snap", None, "feat"),
        P("snap", None),
        P("snap", None),
        P("snap"),
        P("snap", None, None, None),
        P(),
        P(),
        P(),
        P(),
        P(),
        P(),
    )
    return jax.shard_map(
        functools.partial(dispatch, mesh.shape["snap"], mesh.shape["feat"]), mesh=mesh, in_specs=placed, out_specs=P("snap", None, "feat"), check_vma=False
    )
```

```python
import functools
import math

import jax
import jax.numpy as jnp
from jax import lax
from jax.experimental import pallas as pl
from jax.experimental.pallas import tpu as pltpu
from jax.sharding import PartitionSpec as P

HEADS = 8


masked_score = -1e30


def spread_padded(features, tile_block, block_rows, block_cols, slot_count):
    vert_count, feat_width = features.shape
    tile_side = tile_block.shape[1]
    slot_total = tile_block.shape[0]
    block_count = vert_count // tile_side
    blocked = features.reshape(block_count, tile_side, feat_width)
    picked_blocks = blocked[block_cols]
    live_slots = jnp.arange(slot_total, dtype=jnp.int32) < slot_count
    products = jnp.einsum(
        "irc,icf->irf", tile_block, picked_blocks, preferred_element_type=jnp.float32
    )
    products = products * live_slots.astype(jnp.float32)[:, None, None]
    membership = (
        (block_rows[None, :] == jnp.arange(block_count, dtype=jnp.int32)[:, None])
        & live_slots[None, :]
    ).astype(jnp.float32)
    summed = jnp.dot(
        membership,
        products.reshape(slot_total, tile_side * feat_width),
        precision=lax.Precision.HIGHEST,
    )
    return summed.reshape(vert_count, feat_width).astype(jnp.bfloat16)


def attend_local(hidden, query_weight, key_weight, value_weight, out_weight):
    snaps, verts, model_width = hidden.shape
    head_dim = model_width // HEADS
    flat = hidden.reshape(snaps * verts, model_width)

    def project(weight):
        return (
            jnp.dot(flat, weight, preferred_element_type=jnp.float32)
            .astype(jnp.bfloat16)
            .reshape(snaps, verts, HEADS, head_dim)
        )

    query_heads = project(query_weight)
    key_heads = project(key_weight)
    value_heads = project(value_weight)
    scores = jnp.einsum(
        "tvhd,uvhd->vhtu", query_heads, key_heads, preferred_element_type=jnp.float32
    ) * head_dim ** (-0.5)
    causal = (
        jnp.arange(snaps, dtype=jnp.int32)[:, None] >= jnp.arange(snaps, dtype=jnp.int32)[None, :]
    )
    scores = jnp.where(causal, scores, masked_score)
    row_max = jnp.max(scores, axis=-1, keepdims=True)
    lifted = jnp.exp(scores - row_max)
    weights = (lifted / jnp.sum(lifted, axis=-1, keepdims=True)).astype(jnp.bfloat16)
    context = jnp.einsum(
        "vhtu,uvhd->tvhd", weights, value_heads, preferred_element_type=jnp.float32
    ).astype(jnp.bfloat16)
    context = context.reshape(snaps * verts, model_width)
    result = flat.astype(jnp.float32) + jnp.dot(
        context, out_weight, preferred_element_type=jnp.float32
    )
    return result.astype(jnp.bfloat16).reshape(snaps, verts, model_width)


def on_device(
    node_features,
    tile_rows,
    tile_cols,
    tile_counts,
    tile_values,
    layer_one,
    layer_two,
    query_weight,
    key_weight,
    value_weight,
    out_weight,
):
    snap_dev, vert_count, feat_width = node_features.shape
    feat_index = lax.axis_index("feat")

    def spread_all(features):
        spread_pieces = []
        for snapshot in range(snap_dev):
            spread_pieces.append(
                spread_padded(
                    features[snapshot],
                    tile_values[snapshot],
                    tile_rows[snapshot],
                    tile_cols[snapshot],
                    tile_counts[snapshot],
                )
            )
        return jnp.stack(spread_pieces, axis=0)

    def convolve(features, weight):
        spread_rows = spread_all(features).reshape(snap_dev * vert_count, feat_width)
        own_columns = lax.dynamic_slice_in_dim(weight, feat_index * feat_width, feat_width, 1)
        mixed_sum = jnp.dot(
            lax.all_gather(spread_rows, "feat", axis=1, tiled=True),
            own_columns,
            preferred_element_type=jnp.float32,
        )
        mixed_sum = mixed_sum.reshape(snap_dev, vert_count, feat_width)
        return (features.astype(jnp.float32) + jnp.maximum(mixed_sum, 0.0)).astype(jnp.bfloat16)

    hidden_one = convolve(node_features, layer_one)
    hidden_two = convolve(hidden_one, layer_two)
    vertex_rows = lax.all_to_all(
        lax.all_to_all(hidden_two, "snap", split_axis=1, concat_axis=0, tiled=True),
        "feat",
        split_axis=1,
        concat_axis=2,
        tiled=True,
    )
    attended = attend_local(vertex_rows, query_weight, key_weight, value_weight, out_weight)
    return lax.all_to_all(
        lax.all_to_all(attended, "feat", split_axis=2, concat_axis=1, tiled=True),
        "snap",
        split_axis=0,
        concat_axis=1,
        tiled=True,
    )


LANES = 128
CHUNKS = 2
SUBLANES = 8
MESH = pl.DeviceIdType.MESH


def fused_kernel(
    n_snap,
    n_feat,
    rows_hbm,
    cols_hbm,
    counts_hbm,
    feat_ref,
    tiles_ref,
    w_one,
    w_two,
    w_query,
    w_key,
    w_value,
    w_out,
    returned,
    tiles,
    weights,
    away,
    pieces,
    adjacency,
    features,
    hidden_one,
    hidden_two,
    vertex_rows,
    outgoing,
    lending,
    load_sem,
    gather_send,
    gather_recv,
    spread_send,
    spread_recv,
    return_send,
    return_recv,
    heard,
    rows_ref,
    cols_ref,
    counts_ref,
):
    snap_dev, feat_width, vert_count = feat_ref.shape
    slot_total, tile_side, _ = tiles.shape
    block_count = vert_count // tile_side
    snaps, vert_dev, width = vertex_rows.shape
    half_snaps = snaps // 2
    parts = n_feat // snap_dev
    part_rows = vert_count // parts
    head_dim = width // HEADS

    me_snap = lax.axis_index("snap")
    me_feat = lax.axis_index("feat")
    part = me_feat % parts
    local = me_feat // parts
    own = me_snap * snap_dev + local
    half = own // half_snaps
    rank = own % half_snaps
    is_low = half == 0
    is_high = half == 1

    def load(source, target, at):
        copy = pltpu.make_async_copy(source, target, load_sem.at[at])
        copy.start()
        return copy

    def settle(ref, semaphore):
        pltpu.make_async_copy(ref, ref, semaphore).wait()

    barrier = pltpu.get_barrier_semaphore()
    plane = 2
    twin = me_snap + 1 - 2 * (me_snap % 2)
    mates = [(me_feat + step) % n_feat for step in range(1, n_feat)]
    has_below = me_snap >= plane
    has_above = me_snap < n_snap - plane
    column_count = has_below.astype(jnp.int32) + has_above.astype(jnp.int32)

    lead = local * parts + parts - 1

    def signal(semaphore, peer):
        pl.semaphore_signal(semaphore, inc=1, device_id=peer, device_id_type=MESH)

    def tell_column(semaphore):
        @pl.when(has_below)
        def _():
            signal(semaphore, (me_snap - plane, lead))

        @pl.when(has_above)
        def _():
            signal(semaphore, (me_snap + plane, lead))

    def tell_mates(semaphore):
        for mate in mates:
            signal(semaphore, (me_snap, mate))

    leads = part == parts - 1
    lead_count = leads.astype(jnp.int32)
    tell_mates(barrier)
    tell_column(barrier)

    @pl.when(leads)
    def _():
        signal(barrier, (twin, me_feat))

    partner = (me_feat + parts) % n_feat
    away_load = load(feat_ref.at[partner // parts], away, 6)
    own_load = load(feat_ref.at[local], pieces.at[me_feat], 0)
    list_loads = [
        load(ref, kept, 2 + at)
        for at, (ref, kept) in enumerate(
            ((rows_hbm, rows_ref), (cols_hbm, cols_ref), (counts_hbm, counts_ref))
        )
    ]
    tile_load = load(tiles_ref.at[local], tiles, 1)
    weight_list = (w_one, w_two, w_query, w_key, w_value, w_out)
    pl.semaphore_wait(barrier, len(mates) + lead_count * (1 + parts * column_count))

    mate = local * parts + 1 - part
    across = (partner // parts) * parts + 1 - part
    chunk = feat_width // (2 * CHUNKS)
    spans = [pl.ds(at * chunk, chunk) for at in range(CHUNKS)]
    rest = pl.ds(feat_width // 2, feat_width // 2)

    def gather(source, span, at, peer):
        pltpu.make_async_remote_copy(
            src_ref=source.at[span],
            dst_ref=pieces.at[me_feat, span],
            send_sem=gather_send,
            recv_sem=gather_recv.at[at],
            device_id=(me_snap, peer),
            device_id_type=MESH,
        ).start()

    away_load.wait()
    for at in range(CHUNKS):
        gather(away, spans[at], at, partner)
    gather(away, rest, CHUNKS, partner)
    gather(away, rest, CHUNKS, across)
    own_load.wait()
    gather(pieces.at[me_feat], pl.ds(0, feat_width), CHUNKS, mate)

    def relay(at):
        passed = pieces.at[partner, spans[at]]
        settle(passed, gather_recv.at[at])
        pltpu.make_async_remote_copy(
            src_ref=passed,
            dst_ref=passed,
            send_sem=gather_send,
            recv_sem=gather_recv.at[CHUNKS],
            device_id=(me_snap, mate),
            device_id_type=MESH,
        ).start()

    for at, ref in enumerate(weight_list):
        load(ref, weights.at[at], 5)

    hops = n_snap // plane - 2

    @pl.when(leads)
    def _():
        tell_column(heard.at[0])

    tile_load.wait()
    for copy in list_loads:
        copy.wait()
    slot_count = counts_ref[local]
    strip = 2 * SUBLANES
    places = []
    for slot in range(slot_total):
        place = rows_ref[local, slot] * block_count + cols_ref[local, slot]
        place = jnp.where(slot < slot_count, place, -1)
        places.append(jnp.full((strip, tile_side), place, jnp.int32))

    def build(at, carry):
        first = pl.multiple_of(at * strip, strip)
        listed = [
            tiles[slot, pl.ds(first, strip), :].astype(jnp.float32) for slot in range(slot_total)
        ]
        for row in range(block_count):
            for col in range(block_count):
                summed = jnp.zeros((strip, tile_side), jnp.float32)
                for slot in range(slot_total):
                    summed += jnp.where(
                        places[slot] == row * block_count + col, listed[slot], 0.0
                    )
                start = pl.multiple_of(row * tile_side + first, strip)
                adjacency[pl.ds(start, strip), col * tile_side : (col + 1) * tile_side] = (
                    summed.astype(jnp.bfloat16)
                )
        return carry

    strips = tile_side // strip
    lax.fori_loop(0, strips // 2, build, 0)
    for hop in range(hops - 1):

        @pl.when(leads)
        def _():
            pl.semaphore_wait(heard.at[hop], column_count)
            tell_column(heard.at[hop + 1])

    lax.fori_loop(strips // 2, strips, build, 0)

    @pl.when(leads)
    def _():
        pl.semaphore_wait(heard.at[hops - 1], column_count)
        signal(heard.at[hops], (twin, me_feat))

    for at in range(CHUNKS):
        relay(at)

    @pl.when(leads)
    def _():
        pl.semaphore_wait(heard.at[hops], 1)
        tell_mates(heard.at[hops + 1])


    settle(weights, load_sem.at[5])
    settle(pieces.at[:, pl.ds(0, 5 * feat_width // 8)], gather_recv.at[CHUNKS])
    features[...] = jnp.transpose(pieces[...].reshape(width, vert_count))

    def mix(lhs, source, before, weight):
        spread = jnp.dot(lhs, source, preferred_element_type=jnp.float32)
        mixed = jnp.dot(
            spread.astype(jnp.bfloat16), weight, preferred_element_type=jnp.float32
        )
        return (before.astype(jnp.float32) + jnp.maximum(mixed, 0.0)).astype(jnp.bfloat16)

    hidden_one[...] = mix(adjacency[...], features[...], features[...], weights[0])
    pl.semaphore_wait(heard.at[hops + 1], snap_dev - lead_count)

    kept_rows = pl.ds(0, vert_dev - SUBLANES)
    lent_rows = pl.ds(vert_dev - SUBLANES, SUBLANES)
    all_rows = pl.ds(0, vert_dev)

    def spread_to(target_half, peer, rows):
        target = target_half * half_snaps + peer
        pltpu.make_async_remote_copy(
            src_ref=hidden_two.at[peer, rows],
            dst_ref=vertex_rows.at[own, rows],
            send_sem=spread_send.at[target_half],
            recv_sem=spread_recv.at[half],
            device_id=(target // snap_dev, (target % snap_dev) * parts + part),
            device_id_type=MESH,
        ).start()

    def flip(index, mask):
        flipped = 0
        for bit in (4, 2, 1):
            digit = index // bit % 2
            flipped = flipped + bit * (1 - digit if mask & bit else digit)
        return flipped

    def spread_half(target_half, rows):
        for mask in (7, 6, 5, 3, 4, 2, 1):
            spread_to(target_half, flip(rank, mask), rows)

    near = rank % (half_snaps // 2)
    own_rows = pl.ds(pl.multiple_of(part * part_rows, part_rows), part_rows)
    hidden_two[...] = mix(
        adjacency[own_rows, :], hidden_one[...], hidden_one[own_rows, :], weights[1]
    ).reshape(half_snaps, vert_dev, width)

    @pl.when(is_low)
    def _():
        spread_half(0, all_rows)
        for high in (1, 0):
            for mask in (3, 2, 1, 0):
                spread_to(1, high * (half_snaps // 2) + flip(near, mask), kept_rows)
    @pl.when(is_high)
    def _():
        for high in (0, 1):
            for mask in (3, 2, 1, 0):
                spread_to(0, high * (half_snaps // 2) + flip(near, mask), lent_rows)
        spread_half(1, kept_rows)

    vertex_rows[own] = hidden_two[rank]

    groups = vert_dev // SUBLANES
    group_rows = half_snaps * SUBLANES
    pair = 2 * group_rows
    pair_dims = 2 * head_dim
    quads = width // LANES
    quad_pairs = LANES // pair_dims
    half_dev = n_snap // 2

    def split(array):
        array = array.reshape(half_snaps, -1, SUBLANES, width)
        return [array[:, at].reshape(group_rows, width) for at in range(array.shape[1])]

    def project(flat, at):
        return split(jnp.dot(flat, weights[at], preferred_element_type=jnp.float32))

    def score(keys, turned):
        keys = keys.astype(jnp.bfloat16)
        return [
            jnp.dot(
                keys[:, at * LANES : (at + 1) * LANES],
                turned[at],
                preferred_element_type=jnp.float32,
            )
            for at in range(quads)
        ]

    quad_columns = quad_pairs * pair
    row_at = lax.broadcasted_iota(jnp.int32, (group_rows, quad_columns), 0)
    col_at = lax.broadcasted_iota(jnp.int32, (group_rows, quad_columns), 1) % group_rows
    same = row_at % SUBLANES == col_at % SUBLANES
    visible = same & (row_at // SUBLANES <= col_at // SUBLANES)
    factor = head_dim ** (-0.5) * math.log2(math.e)
    none = jnp.zeros((pair_dims, pair), jnp.bfloat16)
    ones = jnp.ones((2 * SUBLANES, group_rows), jnp.bfloat16)

    def masked(keys, queries, seen):
        return [jnp.where(seen, each, masked_score) for each in score(keys, queries)]

    def turn(listed):
        doubled = jnp.concatenate([query for query in listed for _ in range(2)], axis=0)
        turned = jnp.transpose(doubled.astype(jnp.bfloat16))
        turned_head = lax.broadcasted_iota(jnp.int32, turned.shape, 0) // head_dim
        turned_side = lax.broadcasted_iota(jnp.int32, turned.shape, 1) // group_rows
        turned = jnp.where(turned_head % 2 == turned_side % 2, turned, 0.0)
        queries = []
        for at in range(len(listed)):
            columns = turned[:, at * pair : (at + 1) * pair]
            pairs = [
                columns[first : first + pair_dims] for first in range(0, width, pair_dims)
            ]
            queries.append(
                [
                    jnp.concatenate(
                        [
                            jnp.concatenate(
                                [
                                    pairs[quad * quad_pairs + inner] if inner == outer else none
                                    for inner in range(quad_pairs)
                                ],
                                axis=0,
                            )
                            for outer in range(quad_pairs)
                        ],
                        axis=1,
                    )
                    for quad in range(quads)
                ]
            )
        return queries

    def attend(scores_of, values_of, before):
        lane_odd = lax.broadcasted_iota(jnp.int32, (group_rows, width), 1) // head_dim % 2 == 1
        count = len(before)
        contexts = []
        for at in range(count):
            value = jnp.transpose(
                jnp.concatenate([each[at] for each in values_of], axis=0).astype(jnp.bfloat16)
            )
            tail = jnp.concatenate([ones] * len(values_of), axis=1)
            context = []
            for quad in range(quads):
                listed = [each[at][quad] for each in scores_of]
                highest = functools.reduce(
                    jnp.maximum, [jnp.max(each, axis=0, keepdims=True) for each in listed]
                )
                shares = jnp.concatenate(
                    [
                        jnp.exp2((each - highest) * factor).astype(jnp.bfloat16)
                        for each in listed
                    ],
                    axis=0,
                )
                for inner in range(quad_pairs):
                    first = (quad * quad_pairs + inner) * pair_dims
                    product = jnp.dot(
                        jnp.concatenate([value[first : first + pair_dims], tail], axis=0),
                        shares[:, inner * pair : (inner + 1) * pair],
                        preferred_element_type=jnp.float32,
                    )
                    scale = 1.0 / product[pair_dims : pair_dims + 1]
                    context.append((product[:pair_dims] * scale).astype(jnp.bfloat16))
            context = jnp.transpose(jnp.concatenate(context, axis=0))
            contexts.append(jnp.where(lane_odd, context[group_rows:], context[:group_rows]))
        mixed = jnp.dot(
            jnp.concatenate(contexts, axis=0), weights[5], preferred_element_type=jnp.float32
        ).reshape(count, group_rows, width)
        verts = count * SUBLANES
        evolved = jnp.concatenate(
            [
                (before[at] + mixed[at]).reshape(half_snaps, 1, SUBLANES, width)
                for at in range(count)
            ],
            axis=1,
        ).reshape(half_dev, snap_dev, verts, width)
        low = lax.broadcasted_iota(jnp.int32, (half_dev * verts, LANES), 1) < feat_width
        outs = []
        for at in range(0, n_feat, 2):
            lanes = slice(at * feat_width, (at + 2) * feat_width)
            first = evolved[:, 0, :, lanes].reshape(half_dev * verts, LANES)
            second = evolved[:, 1, :, lanes].reshape(half_dev * verts, LANES)
            even = jnp.where(low, first, pltpu.roll(second, feat_width, 1))
            odd = jnp.where(low, pltpu.roll(first, feat_width, 1), second)
            outs += [each.reshape(half_dev, verts, LANES) for each in (even, odd)]
        return outs

    total = half_dev * n_feat
    me = (me_snap % half_dev) * n_feat + me_feat

    def hand_back(source, target_half, peer, rows, source_rows, at):
        pltpu.make_async_remote_copy(
            src_ref=source.at[peer % n_feat, peer // n_feat, source_rows],
            dst_ref=returned.at[part, rank, rows],
            send_sem=return_send.at[at],
            recv_sem=return_recv.at[at],
            device_id=(target_half * half_dev + peer // n_feat, peer % n_feat),
            device_id_type=MESH,
        ).start()

    masks = (14, 15, 12, 13, 10, 11, 6, 7, 8, 9, 4, 5, 2, 3, 1, 0)
    mirrored = [
        flip(me // 2, mask // 2) * 2 + (1 - me % 2 if mask % 2 else me % 2) for mask in masks
    ]

    def own_part(rows):
        flat = rows.reshape(half_snaps * vert_dev, width)
        return project(flat, 2), project(flat, 3), project(flat, 4), split(flat.astype(jnp.float32))

    @pl.when(is_low)
    def _():
        settle(vertex_rows.at[pl.ds(0, half_snaps - 1)], spread_recv.at[0])
        queries, keys, values, before = own_part(vertex_rows[pl.ds(0, half_snaps)])
        queries = turn(queries)
        scores = [masked(keys[at], queries[at], visible) for at in range(groups)]
        for at, out in enumerate(attend([scores], [values], before)):
            outgoing[at] = out.astype(jnp.bfloat16)
        for peer in mirrored[:-1]:
            hand_back(outgoing, 0, peer, all_rows, all_rows, 0)
        load(outgoing.at[me_feat, me_snap % half_dev], returned.at[part, rank], 0)
        settle(vertex_rows.at[pl.ds(0, half_snaps), lent_rows], spread_recv.at[1])
        lent = vertex_rows[
            pl.ds(half_snaps, half_snaps), pl.ds(vert_dev - 2 * SUBLANES, 2 * SUBLANES)
        ].astype(jnp.float32)[:, SUBLANES:]
        flat = lent.reshape(group_rows, width)
        rounded = flat.astype(jnp.bfloat16)
        turned = turn(project(rounded, 2))
        scores = [masked(project(rounded, 3)[0], turned[0], visible)]
        scores_low = [masked(keys[groups - 1], turned[0], same)]
        outs = attend(
            [scores_low, scores], [values[groups - 1 :], project(rounded, 4)], [flat]
        )
        for at, out in enumerate(outs):
            lending[at] = out.astype(jnp.bfloat16)
        for peer in mirrored:
            hand_back(lending, 1, peer, lent_rows, pl.ds(0, SUBLANES), 1)
        settle(hidden_two.at[:, kept_rows], spread_send.at[1])
        settle(hidden_two.at[pl.ds(0, half_snaps - 1)], spread_send.at[0])
        pltpu.make_async_copy(
            outgoing.at[0, 0], returned.at[part, rank], load_sem.at[0]
        ).wait()
        everyone = outgoing.reshape(total, vert_dev, LANES).at[pl.ds(0, total - 1)]
        settle(everyone, return_recv.at[0])
        settle(everyone, return_send.at[0])
        settle(lending, return_send.at[1])

    @pl.when(is_high)
    def _():
        settle(vertex_rows.at[pl.ds(0, half_snaps - 1), kept_rows], spread_recv.at[1])
        queries, keys, values, before = own_part(vertex_rows[pl.ds(half_snaps, half_snaps)])
        queries = turn(queries[:-1])
        scores = [masked(keys[at], queries[at], visible) for at in range(groups - 1)]
        settle(vertex_rows.at[pl.ds(0, half_snaps), kept_rows], spread_recv.at[0])
        flat_low = vertex_rows[pl.ds(0, half_snaps)].reshape(half_snaps * vert_dev, width)
        keys_low, values_low = project(flat_low, 3), project(flat_low, 4)
        scores_low = [
            masked(keys_low[at], queries[at], same) for at in range(groups - 1)
        ]
        outs = attend([scores_low, scores], [values_low, values], before[:-1])
        for at, out in enumerate(outs):
            outgoing[at, :, kept_rows] = out.astype(jnp.bfloat16)
        for peer in mirrored[:-1]:
            hand_back(outgoing, 1, peer, kept_rows, kept_rows, 0)
        own_copy = load(
            outgoing.at[me_feat, me_snap % half_dev, kept_rows],
            returned.at[part, rank, kept_rows],
            0,
        )
        settle(hidden_two.at[:, lent_rows], spread_send.at[0])
        settle(hidden_two.at[pl.ds(0, half_snaps - 1), kept_rows], spread_send.at[1])
        own_copy.wait()
        everyone = outgoing.reshape(total, vert_dev, LANES).at[pl.ds(0, total - 1), kept_rows]
        settle(everyone, return_recv.at[0])
        settle(lending, return_recv.at[1])
        settle(everyone, return_send.at[0])

    settle(pieces.at[pl.ds(0, n_feat - 1)], gather_send)


def on_device_fused(n_snap, n_feat, *operands):
    node_features, _, _, _, tile_values, layer_one = operands[:6]
    snap_dev, vert_count, feat_width = node_features.shape
    _, slot_total, tile_side, _ = tile_values.shape
    width = layer_one.shape[0]
    parts = n_feat // snap_dev
    snaps = n_snap * snap_dev
    half_snaps = snaps // 2
    vert_dev = vert_count // (parts * half_snaps)
    kept = jnp.bfloat16
    result = pl.pallas_call(
        functools.partial(fused_kernel, n_snap, n_feat),
        out_shape=pltpu.VMEM((parts, half_snaps, vert_dev, LANES), kept),
        in_specs=[pl.BlockSpec(memory_space=pltpu.HBM)] * 11,
        out_specs=pl.BlockSpec(memory_space=pltpu.VMEM),
        scratch_shapes=[
            pltpu.VMEM((slot_total, tile_side, tile_side), kept),
            pltpu.VMEM((6, width, width), kept),
            pltpu.VMEM((feat_width, vert_count), kept),
            pltpu.VMEM((n_feat, feat_width, vert_count), kept),
            pltpu.VMEM((vert_count, vert_count), kept),
            pltpu.VMEM((vert_count, width), kept),
            pltpu.VMEM((vert_count, width), kept),
            pltpu.VMEM((half_snaps, vert_dev, width), kept),
            pltpu.VMEM((snaps, vert_dev, width), kept),
            pltpu.VMEM((n_feat, n_snap // 2, vert_dev, LANES), kept),
            pltpu.VMEM((n_feat, n_snap // 2, SUBLANES, LANES), kept),
            pltpu.SemaphoreType.DMA((7,)),
            pltpu.SemaphoreType.DMA,
            pltpu.SemaphoreType.DMA((CHUNKS + 1,)),
            pltpu.SemaphoreType.DMA((2,)),
            pltpu.SemaphoreType.DMA((2,)),
            pltpu.SemaphoreType.DMA((2,)),
            pltpu.SemaphoreType.DMA((2,)),
            pltpu.SemaphoreType.REGULAR((n_snap // 2,)),
            pltpu.SMEM((snap_dev, slot_total), jnp.int32),
            pltpu.SMEM((snap_dev, slot_total), jnp.int32),
            pltpu.SMEM((snap_dev,), jnp.int32),
        ],
        compiler_params=pltpu.CompilerParams(collective_id=0, has_side_effects=True),
    )(*operands[1:4], node_features.transpose(0, 2, 1), *operands[4:])
    result = jnp.transpose(result.reshape(vert_count, LANES))
    return result.reshape(snap_dev, feat_width, vert_count).transpose(0, 2, 1)


def dispatch(n_snap, n_feat, *operands):
    snap_dev, vert_count, feat_width = operands[0].shape
    slot_total = operands[4].shape[1]
    snaps = n_snap * snap_dev
    fits = (
        snap_dev == 2
        and 2 * feat_width == LANES
        and n_feat == 2 * snap_dev
        and n_snap >= 8
        and n_snap % 4 == 0
        and vert_count % (n_feat // snap_dev * snaps * SUBLANES) == 0
        and snaps * SUBLANES == LANES
        and slot_total <= 16
        and vert_count <= 1024
    )
    if fits:
        return on_device_fused(n_snap, n_feat, *operands)
    return on_device(*operands)


def solution(mesh):
    placed = (
        P("snap", None, "feat"),
        P("snap", None),
        P("snap", None),
        P("snap"),
        P("snap", None, None, None),
        P(),
        P(),
        P(),
        P(),
        P(),
        P(),
    )
    return jax.shard_map(
        functools.partial(dispatch, mesh.shape["snap"], mesh.shape["feat"]), mesh=mesh, in_specs=placed, out_specs=P("snap", None, "feat"), check_vma=False
    )
```

```python
import functools
import math

import jax
import jax.numpy as jnp
from jax import lax
from jax.experimental import pallas as pl
from jax.experimental.pallas import tpu as pltpu
from jax.sharding import PartitionSpec as P

HEADS = 8


masked_score = -1e30


def spread_padded(features, tile_block, block_rows, block_cols, slot_count):
    vert_count, feat_width = features.shape
    tile_side = tile_block.shape[1]
    slot_total = tile_block.shape[0]
    block_count = vert_count // tile_side
    blocked = features.reshape(block_count, tile_side, feat_width)
    picked_blocks = blocked[block_cols]
    live_slots = jnp.arange(slot_total, dtype=jnp.int32) < slot_count
    products = jnp.einsum(
        "irc,icf->irf", tile_block, picked_blocks, preferred_element_type=jnp.float32
    )
    products = products * live_slots.astype(jnp.float32)[:, None, None]
    membership = (
        (block_rows[None, :] == jnp.arange(block_count, dtype=jnp.int32)[:, None])
        & live_slots[None, :]
    ).astype(jnp.float32)
    summed = jnp.dot(
        membership,
        products.reshape(slot_total, tile_side * feat_width),
        precision=lax.Precision.HIGHEST,
    )
    return summed.reshape(vert_count, feat_width).astype(jnp.bfloat16)


def attend_local(hidden, query_weight, key_weight, value_weight, out_weight):
    snaps, verts, model_width = hidden.shape
    head_dim = model_width // HEADS
    flat = hidden.reshape(snaps * verts, model_width)

    def project(weight):
        return (
            jnp.dot(flat, weight, preferred_element_type=jnp.float32)
            .astype(jnp.bfloat16)
            .reshape(snaps, verts, HEADS, head_dim)
        )

    query_heads = project(query_weight)
    key_heads = project(key_weight)
    value_heads = project(value_weight)
    scores = jnp.einsum(
        "tvhd,uvhd->vhtu", query_heads, key_heads, preferred_element_type=jnp.float32
    ) * head_dim ** (-0.5)
    causal = (
        jnp.arange(snaps, dtype=jnp.int32)[:, None] >= jnp.arange(snaps, dtype=jnp.int32)[None, :]
    )
    scores = jnp.where(causal, scores, masked_score)
    row_max = jnp.max(scores, axis=-1, keepdims=True)
    lifted = jnp.exp(scores - row_max)
    weights = (lifted / jnp.sum(lifted, axis=-1, keepdims=True)).astype(jnp.bfloat16)
    context = jnp.einsum(
        "vhtu,uvhd->tvhd", weights, value_heads, preferred_element_type=jnp.float32
    ).astype(jnp.bfloat16)
    context = context.reshape(snaps * verts, model_width)
    result = flat.astype(jnp.float32) + jnp.dot(
        context, out_weight, preferred_element_type=jnp.float32
    )
    return result.astype(jnp.bfloat16).reshape(snaps, verts, model_width)


def on_device(
    node_features,
    tile_rows,
    tile_cols,
    tile_counts,
    tile_values,
    layer_one,
    layer_two,
    query_weight,
    key_weight,
    value_weight,
    out_weight,
):
    snap_dev, vert_count, feat_width = node_features.shape
    feat_index = lax.axis_index("feat")

    def spread_all(features):
        spread_pieces = []
        for snapshot in range(snap_dev):
            spread_pieces.append(
                spread_padded(
                    features[snapshot],
                    tile_values[snapshot],
                    tile_rows[snapshot],
                    tile_cols[snapshot],
                    tile_counts[snapshot],
                )
            )
        return jnp.stack(spread_pieces, axis=0)

    def convolve(features, weight):
        spread_rows = spread_all(features).reshape(snap_dev * vert_count, feat_width)
        own_columns = lax.dynamic_slice_in_dim(weight, feat_index * feat_width, feat_width, 1)
        mixed_sum = jnp.dot(
            lax.all_gather(spread_rows, "feat", axis=1, tiled=True),
            own_columns,
            preferred_element_type=jnp.float32,
        )
        mixed_sum = mixed_sum.reshape(snap_dev, vert_count, feat_width)
        return (features.astype(jnp.float32) + jnp.maximum(mixed_sum, 0.0)).astype(jnp.bfloat16)

    hidden_one = convolve(node_features, layer_one)
    hidden_two = convolve(hidden_one, layer_two)
    vertex_rows = lax.all_to_all(
        lax.all_to_all(hidden_two, "snap", split_axis=1, concat_axis=0, tiled=True),
        "feat",
        split_axis=1,
        concat_axis=2,
        tiled=True,
    )
    attended = attend_local(vertex_rows, query_weight, key_weight, value_weight, out_weight)
    return lax.all_to_all(
        lax.all_to_all(attended, "feat", split_axis=2, concat_axis=1, tiled=True),
        "snap",
        split_axis=0,
        concat_axis=1,
        tiled=True,
    )


LANES = 128
CHUNKS = 2
LENT = (1, 2)
SUBLANES = 8
MESH = pl.DeviceIdType.MESH


def fused_kernel(
    n_snap,
    n_feat,
    rows_hbm,
    cols_hbm,
    counts_hbm,
    feat_ref,
    tiles_ref,
    w_one,
    w_two,
    w_query,
    w_key,
    w_value,
    w_out,
    returned,
    tiles,
    weights,
    away,
    pieces,
    adjacency,
    features,
    hidden_one,
    hidden_two,
    vertex_rows,
    outgoing,
    lending,
    load_sem,
    gather_send,
    gather_recv,
    spread_send,
    spread_recv,
    return_send,
    return_recv,
    heard,
    rows_ref,
    cols_ref,
    counts_ref,
):
    snap_dev, feat_width, vert_count = feat_ref.shape
    slot_total, tile_side, _ = tiles.shape
    block_count = vert_count // tile_side
    snaps, vert_dev, width = vertex_rows.shape
    half_snaps = snaps // 2
    parts = n_feat // snap_dev
    part_rows = vert_count // parts
    head_dim = width // HEADS

    me_snap = lax.axis_index("snap")
    me_feat = lax.axis_index("feat")
    part = me_feat % parts
    local = me_feat // parts
    own = me_snap * snap_dev + local
    half = own // half_snaps
    rank = own % half_snaps
    is_low = half == 0
    is_high = half == 1

    def load(source, target, at):
        copy = pltpu.make_async_copy(source, target, load_sem.at[at])
        copy.start()
        return copy

    def settle(ref, semaphore):
        pltpu.make_async_copy(ref, ref, semaphore).wait()

    barrier = pltpu.get_barrier_semaphore()
    plane = 2
    twin = me_snap + 1 - 2 * (me_snap % 2)
    mates = [(me_feat + step) % n_feat for step in range(1, n_feat)]
    has_below = me_snap >= plane
    has_above = me_snap < n_snap - plane
    column_count = has_below.astype(jnp.int32) + has_above.astype(jnp.int32)

    lead = local * parts + parts - 1

    def signal(semaphore, peer):
        pl.semaphore_signal(semaphore, inc=1, device_id=peer, device_id_type=MESH)

    def tell_column(semaphore):
        @pl.when(has_below)
        def _():
            signal(semaphore, (me_snap - plane, lead))

        @pl.when(has_above)
        def _():
            signal(semaphore, (me_snap + plane, lead))

    def tell_mates(semaphore):
        for mate in mates:
            signal(semaphore, (me_snap, mate))

    leads = part == parts - 1
    lead_count = leads.astype(jnp.int32)
    tell_mates(barrier)

    @pl.when(leads)
    def _():
        signal(barrier, (twin, me_feat))

    @pl.when(leads | (column_count == 1))
    def _():
        tell_column(barrier)

    level = me_snap // plane
    near_end = (level == 1).astype(jnp.int32) + (level == n_snap // plane - 2).astype(jnp.int32)
    partner = (me_feat + parts) % n_feat
    away_load = load(feat_ref.at[partner // parts], away, 6)
    own_load = load(feat_ref.at[local], pieces.at[me_feat], 0)
    list_loads = [
        load(ref, kept, 2 + at)
        for at, (ref, kept) in enumerate(
            ((rows_hbm, rows_ref), (cols_hbm, cols_ref), (counts_hbm, counts_ref))
        )
    ]
    tile_load = load(tiles_ref.at[local], tiles, 1)
    weight_list = (w_one, w_two, w_query, w_key, w_value, w_out)
    pl.semaphore_wait(barrier, len(mates) + lead_count * (1 + column_count + near_end))

    mate = local * parts + 1 - part
    across = (partner // parts) * parts + 1 - part
    chunk = feat_width // CHUNKS
    spans = [pl.ds(at * chunk, chunk) for at in range(CHUNKS)]
    whole = pl.ds(0, feat_width)

    def gather(source, span, at, peer):
        pltpu.make_async_remote_copy(
            src_ref=source.at[span],
            dst_ref=pieces.at[me_feat, span],
            send_sem=gather_send,
            recv_sem=gather_recv.at[at],
            device_id=(me_snap, peer),
            device_id_type=MESH,
        ).start()

    away_load.wait()

    @pl.when(leads)
    def _():
        for at in range(CHUNKS):
            gather(away, spans[at], at, partner)

    @pl.when(part == 0)
    def _():
        gather(away, whole, CHUNKS, partner)
        gather(away, whole, CHUNKS, across)

    own_load.wait()
    gather(pieces.at[me_feat], whole, CHUNKS, mate)

    def relay(at):
        passed = pieces.at[partner, spans[at]]
        settle(passed, gather_recv.at[at])
        pltpu.make_async_remote_copy(
            src_ref=passed,
            dst_ref=passed,
            send_sem=gather_send,
            recv_sem=gather_recv.at[CHUNKS],
            device_id=(me_snap, mate),
            device_id_type=MESH,
        ).start()

    for at, ref in enumerate(weight_list):
        load(ref, weights.at[at], 5)

    hops = n_snap // plane - 2

    @pl.when(leads)
    def _():
        tell_column(heard.at[0])

    tile_load.wait()
    for copy in list_loads:
        copy.wait()
    slot_count = counts_ref[local]
    strip = 2 * SUBLANES
    places = []
    for slot in range(slot_total):
        place = rows_ref[local, slot] * block_count + cols_ref[local, slot]
        place = jnp.where(slot < slot_count, place, -1)
        places.append(jnp.full((strip, tile_side), place, jnp.int32))

    def build(at, carry):
        first = pl.multiple_of(at * strip, strip)
        listed = [
            tiles[slot, pl.ds(first, strip), :].astype(jnp.float32) for slot in range(slot_total)
        ]
        for row in range(block_count):
            for col in range(block_count):
                summed = jnp.zeros((strip, tile_side), jnp.float32)
                for slot in range(slot_total):
                    summed += jnp.where(
                        places[slot] == row * block_count + col, listed[slot], 0.0
                    )
                start = pl.multiple_of(row * tile_side + first, strip)
                adjacency[pl.ds(start, strip), col * tile_side : (col + 1) * tile_side] = (
                    summed.astype(jnp.bfloat16)
                )
        return carry

    strips = tile_side // strip
    lax.fori_loop(0, strips // 2, build, 0)
    lax.fori_loop(strips // 2, strips, build, 0)
    for hop in range(hops - 1):

        @pl.when(leads)
        def _():
            pl.semaphore_wait(heard.at[hop], column_count)
            tell_column(heard.at[hop + 1])


    @pl.when(leads)
    def _():
        pl.semaphore_wait(heard.at[hops - 1], column_count)
        signal(heard.at[hops], (twin, me_feat))

    @pl.when(leads)
    def _():
        for at in range(CHUNKS):
            relay(at)
        pl.semaphore_wait(heard.at[hops], 1)
        tell_mates(heard.at[hops + 1])


    settle(weights, load_sem.at[5])

    @pl.when(leads)
    def _():
        settle(pieces.at[pl.ds(0, n_feat - 2)], gather_recv.at[CHUNKS])

    @pl.when(part == 0)
    def _():
        settle(pieces.at[pl.ds(0, n_feat - 1)], gather_recv.at[CHUNKS])

    features[...] = jnp.transpose(pieces[...].reshape(width, vert_count))

    def mix(lhs, source, before, weight):
        spread = jnp.dot(lhs, source, preferred_element_type=jnp.float32)
        mixed = jnp.dot(
            spread.astype(jnp.bfloat16), weight, preferred_element_type=jnp.float32
        )
        return (before.astype(jnp.float32) + jnp.maximum(mixed, 0.0)).astype(jnp.bfloat16)

    hidden_one[...] = mix(adjacency[...], features[...], features[...], weights[0])
    pl.semaphore_wait(heard.at[hops + 1], snap_dev - lead_count)

    side = half_snaps // 2
    far = rank // side
    keeps = [vert_dev - each * SUBLANES for each in LENT]
    lends = [each * SUBLANES for each in LENT]
    kept_rows = [pl.ds(0, each) for each in keeps]
    lent_rows = [pl.ds(keep, lend) for keep, lend in zip(keeps, lends)]
    all_rows = pl.ds(0, vert_dev)

    def spread_to(target_half, peer, rows):
        target = target_half * half_snaps + peer
        pltpu.make_async_remote_copy(
            src_ref=hidden_two.at[peer, rows],
            dst_ref=vertex_rows.at[own, rows],
            send_sem=spread_send.at[target_half],
            recv_sem=spread_recv.at[half],
            device_id=(target // snap_dev, (target % snap_dev) * parts + part),
            device_id_type=MESH,
        ).start()

    def flip(index, mask):
        flipped = 0
        for bit in (4, 2, 1):
            digit = index // bit % 2
            flipped = flipped + bit * (1 - digit if mask & bit else digit)
        return flipped

    def spread_half(target_half, rows):
        for mask in (7, 6, 5, 3, 4, 2, 1):
            spread_to(target_half, flip(rank, mask), rows)

    near = rank % (half_snaps // 2)
    own_rows = pl.ds(pl.multiple_of(part * part_rows, part_rows), part_rows)
    hidden_two[...] = mix(
        adjacency[own_rows, :], hidden_one[...], hidden_one[own_rows, :], weights[1]
    ).reshape(half_snaps, vert_dev, width)

    @pl.when(is_low)
    def _():
        spread_half(0, all_rows)
        for high in (1, 0):
            for mask in (3, 2, 1, 0):
                spread_to(1, high * side + flip(near, mask), kept_rows[high])
    @pl.when(is_high)
    def _():
        for high in (0, 1):
            for mask in (3, 2, 1, 0):
                spread_to(0, high * side + flip(near, mask), lent_rows[high])

    for high in range(2):

        @pl.when(is_high & (far == high))
        def _():
            for mask in (7, 6, 5, 3, 4, 2, 1):
                peer_high = high if mask < 4 else 1 - high
                spread_to(
                    1, peer_high * side + flip(near, mask % 4), kept_rows[peer_high]
                )


    vertex_rows[own] = hidden_two[rank]

    groups = vert_dev // SUBLANES
    group_rows = half_snaps * SUBLANES
    pair = 2 * group_rows
    pair_dims = 2 * head_dim
    quads = width // LANES
    quad_pairs = LANES // pair_dims
    half_dev = n_snap // 2

    def split(array):
        array = array.reshape(half_snaps, -1, SUBLANES, width)
        return [array[:, at].reshape(group_rows, width) for at in range(array.shape[1])]

    def project(flat, at):
        return split(jnp.dot(flat, weights[at], preferred_element_type=jnp.float32))

    def score(keys, turned):
        keys = keys.astype(jnp.bfloat16)
        return [
            jnp.dot(
                keys[:, at * LANES : (at + 1) * LANES],
                turned[at],
                preferred_element_type=jnp.float32,
            )
            for at in range(quads)
        ]

    quad_columns = quad_pairs * pair
    row_at = lax.broadcasted_iota(jnp.int32, (group_rows, quad_columns), 0)
    col_at = lax.broadcasted_iota(jnp.int32, (group_rows, quad_columns), 1) % group_rows
    same = row_at % SUBLANES == col_at % SUBLANES
    visible = same & (row_at // SUBLANES <= col_at // SUBLANES)
    factor = head_dim ** (-0.5) * math.log2(math.e)
    none = jnp.zeros((pair_dims, pair), jnp.bfloat16)
    ones = jnp.ones((2 * SUBLANES, group_rows), jnp.bfloat16)

    def masked(keys, queries, seen):
        return [jnp.where(seen, each, masked_score) for each in score(keys, queries)]

    def turn(listed):
        doubled = jnp.concatenate([query for query in listed for _ in range(2)], axis=0)
        turned = jnp.transpose(doubled.astype(jnp.bfloat16))
        turned_head = lax.broadcasted_iota(jnp.int32, turned.shape, 0) // head_dim
        turned_side = lax.broadcasted_iota(jnp.int32, turned.shape, 1) // group_rows
        turned = jnp.where(turned_head % 2 == turned_side % 2, turned, 0.0)
        queries = []
        for at in range(len(listed)):
            columns = turned[:, at * pair : (at + 1) * pair]
            pairs = [
                columns[first : first + pair_dims] for first in range(0, width, pair_dims)
            ]
            queries.append(
                [
                    jnp.concatenate(
                        [
                            jnp.concatenate(
                                [
                                    pairs[quad * quad_pairs + inner] if inner == outer else none
                                    for inner in range(quad_pairs)
                                ],
                                axis=0,
                            )
                            for outer in range(quad_pairs)
                        ],
                        axis=1,
                    )
                    for quad in range(quads)
                ]
            )
        return queries

    def attend(scores_of, values_of, before):
        lane_odd = lax.broadcasted_iota(jnp.int32, (group_rows, width), 1) // head_dim % 2 == 1
        count = len(before)
        contexts = []
        for at in range(count):
            value = jnp.transpose(
                jnp.concatenate([each[at] for each in values_of], axis=0).astype(jnp.bfloat16)
            )
            tail = jnp.concatenate([ones] * len(values_of), axis=1)
            context = []
            for quad in range(quads):
                listed = [each[at][quad] for each in scores_of]
                highest = functools.reduce(
                    jnp.maximum, [jnp.max(each, axis=0, keepdims=True) for each in listed]
                )
                shares = jnp.concatenate(
                    [
                        jnp.exp2((each - highest) * factor).astype(jnp.bfloat16)
                        for each in listed
                    ],
                    axis=0,
                )
                for inner in range(quad_pairs):
                    first = (quad * quad_pairs + inner) * pair_dims
                    product = jnp.dot(
                        jnp.concatenate([value[first : first + pair_dims], tail], axis=0),
                        shares[:, inner * pair : (inner + 1) * pair],
                        preferred_element_type=jnp.float32,
                    )
                    scale = 1.0 / product[pair_dims : pair_dims + 1]
                    context.append((product[:pair_dims] * scale).astype(jnp.bfloat16))
            context = jnp.transpose(jnp.concatenate(context, axis=0))
            contexts.append(jnp.where(lane_odd, context[group_rows:], context[:group_rows]))
        mixed = jnp.dot(
            jnp.concatenate(contexts, axis=0), weights[5], preferred_element_type=jnp.float32
        ).reshape(count, group_rows, width)
        verts = count * SUBLANES
        evolved = jnp.concatenate(
            [
                (before[at] + mixed[at]).reshape(half_snaps, 1, SUBLANES, width)
                for at in range(count)
            ],
            axis=1,
        ).reshape(half_dev, snap_dev, verts, width)
        low = lax.broadcasted_iota(jnp.int32, (half_dev * verts, LANES), 1) < feat_width
        outs = []
        for at in range(0, n_feat, 2):
            lanes = slice(at * feat_width, (at + 2) * feat_width)
            first = evolved[:, 0, :, lanes].reshape(half_dev * verts, LANES)
            second = evolved[:, 1, :, lanes].reshape(half_dev * verts, LANES)
            even = jnp.where(low, first, pltpu.roll(second, feat_width, 1))
            odd = jnp.where(low, pltpu.roll(first, feat_width, 1), second)
            outs += [each.reshape(half_dev, verts, LANES) for each in (even, odd)]
        return outs

    total = half_dev * n_feat
    outgoing_rows = outgoing.reshape(total * vert_dev, LANES)
    me = (me_snap % half_dev) * n_feat + me_feat

    def hand_back(source, target_half, peer, rows, source_rows, at):
        pltpu.make_async_remote_copy(
            src_ref=source.at[peer % n_feat, peer // n_feat, source_rows],
            dst_ref=returned.at[part, rank, rows],
            send_sem=return_send.at[at],
            recv_sem=return_recv.at[at],
            device_id=(target_half * half_dev + peer // n_feat, peer % n_feat),
            device_id_type=MESH,
        ).start()

    masks = (14, 15, 12, 13, 10, 11, 6, 7, 8, 9, 4, 5, 2, 3, 1, 0)
    mirrored = [
        flip(me // 2, mask // 2) * 2 + (1 - me % 2 if mask % 2 else me % 2) for mask in masks
    ]

    def own_part(rows):
        flat = rows.reshape(half_snaps * vert_dev, width)
        return project(flat, 2), project(flat, 3), project(flat, 4), split(flat.astype(jnp.float32))

    @pl.when(is_low)
    def _():
        settle(vertex_rows.at[pl.ds(0, half_snaps - 1)], spread_recv.at[0])
        queries, keys, values, before = own_part(vertex_rows[pl.ds(0, half_snaps)])
        queries = turn(queries)
        scores = [masked(keys[at], queries[at], visible) for at in range(groups)]
        for at, out in enumerate(attend([scores], [values], before)):
            outgoing[at] = out.astype(jnp.bfloat16)
        for peer in mirrored[:-1]:
            hand_back(outgoing, 0, peer, all_rows, all_rows, 0)
        load(outgoing.at[me_feat, me_snap % half_dev], returned.at[part, rank], 0)
        for high in range(2):

            @pl.when(far == high)
            def _():
                count = LENT[high]
                settle(
                    vertex_rows.at[pl.ds(0, half_snaps), lent_rows[high]], spread_recv.at[1]
                )
                base = keeps[high] // (2 * SUBLANES) * 2 * SUBLANES
                lent = vertex_rows[
                    pl.ds(half_snaps, half_snaps), pl.ds(base, vert_dev - base)
                ].astype(jnp.float32)[:, keeps[high] - base :]
                flats = split(lent)
                rounded = jnp.concatenate(flats, axis=0).astype(jnp.bfloat16)

                def lent_part(at):
                    out = jnp.dot(rounded, weights[at], preferred_element_type=jnp.float32)
                    return [
                        out[each * group_rows : (each + 1) * group_rows]
                        for each in range(count)
                    ]

                turned = turn(lent_part(2))
                lent_keys = lent_part(3)
                scores = [masked(lent_keys[at], turned[at], visible) for at in range(count)]
                scores_low = [
                    masked(keys[groups - count + at], turned[at], same)
                    for at in range(count)
                ]
                outs = attend(
                    [scores_low, scores], [values[groups - count :], lent_part(4)], flats
                )
                for at, out in enumerate(outs):
                    lending[at, :, pl.ds(0, lends[high])] = out.astype(jnp.bfloat16)
                for peer in mirrored:
                    hand_back(lending, 1, peer, lent_rows[high], pl.ds(0, lends[high]), 1)
                settle(outgoing_rows.at[pl.ds(0, total * lends[high])], return_send.at[1])

        settle(hidden_one.at[pl.ds(0, side * sum(keeps))], spread_send.at[1])
        settle(hidden_two.at[pl.ds(0, half_snaps - 1)], spread_send.at[0])
        pltpu.make_async_copy(
            outgoing.at[0, 0], returned.at[part, rank], load_sem.at[0]
        ).wait()
        everyone = outgoing_rows.at[pl.ds(0, (total - 1) * vert_dev)]
        settle(everyone, return_recv.at[0])
        settle(everyone, return_send.at[0])

    for high in range(2):

        @pl.when(is_high & (far == high))
        def _():
            keep = keeps[high]
            count = groups - LENT[high]
            kept = kept_rows[high]
            settle(vertex_rows.at[pl.ds(0, half_snaps - 1), kept], spread_recv.at[1])
            queries, keys, values, before = own_part(
                vertex_rows[pl.ds(half_snaps, half_snaps)]
            )
            queries = turn(queries[:count])
            scores = [masked(keys[at], queries[at], visible) for at in range(count)]
            settle(vertex_rows.at[pl.ds(0, half_snaps), kept], spread_recv.at[0])
            flat_low = vertex_rows[pl.ds(0, half_snaps)].reshape(half_snaps * vert_dev, width)
            keys_low, values_low = project(flat_low, 3), project(flat_low, 4)
            scores_low = [masked(keys_low[at], queries[at], same) for at in range(count)]
            outs = attend([scores_low, scores], [values_low, values], before[:count])
            for at, out in enumerate(outs):
                outgoing[at, :, kept] = out.astype(jnp.bfloat16)
            for peer in mirrored[:-1]:
                hand_back(outgoing, 1, peer, kept, kept, 0)
            own_copy = load(
                outgoing.at[me_feat, me_snap % half_dev, kept], returned.at[part, rank, kept], 0
            )
            settle(hidden_one.at[pl.ds(0, side * sum(lends))], spread_send.at[0])
            settle(
                hidden_one.at[pl.ds(0, side * sum(keeps) - keep)], spread_send.at[1]
            )
            own_copy.wait()
            settle(
                outgoing_rows.at[pl.ds(0, total // 2 * sum(keeps) - keep)], return_recv.at[0]
            )
            settle(
                outgoing_rows.at[pl.ds(0, total // 2 * sum(lends))], return_recv.at[1]
            )
            settle(outgoing_rows.at[pl.ds(0, (total - 1) * keep)], return_send.at[0])

    settle(pieces.at[pl.ds(0, n_feat - 1)], gather_send)


def on_device_fused(n_snap, n_feat, *operands):
    node_features, _, _, _, tile_values, layer_one = operands[:6]
    snap_dev, vert_count, feat_width = node_features.shape
    _, slot_total, tile_side, _ = tile_values.shape
    width = layer_one.shape[0]
    parts = n_feat // snap_dev
    snaps = n_snap * snap_dev
    half_snaps = snaps // 2
    vert_dev = vert_count // (parts * half_snaps)
    kept = jnp.bfloat16
    result = pl.pallas_call(
        functools.partial(fused_kernel, n_snap, n_feat),
        out_shape=pltpu.VMEM((parts, half_snaps, vert_dev, LANES), kept),
        in_specs=[pl.BlockSpec(memory_space=pltpu.HBM)] * 11,
        out_specs=pl.BlockSpec(memory_space=pltpu.VMEM),
        scratch_shapes=[
            pltpu.VMEM((slot_total, tile_side, tile_side), kept),
            pltpu.VMEM((6, width, width), kept),
            pltpu.VMEM((feat_width, vert_count), kept),
            pltpu.VMEM((n_feat, feat_width, vert_count), kept),
            pltpu.VMEM((vert_count, vert_count), kept),
            pltpu.VMEM((vert_count, width), kept),
            pltpu.VMEM((vert_count, width), kept),
            pltpu.VMEM((half_snaps, vert_dev, width), kept),
            pltpu.VMEM((snaps, vert_dev, width), kept),
            pltpu.VMEM((n_feat, n_snap // 2, vert_dev, LANES), kept),
            pltpu.VMEM((n_feat, n_snap // 2, max(LENT) * SUBLANES, LANES), kept),
            pltpu.SemaphoreType.DMA((7,)),
            pltpu.SemaphoreType.DMA,
            pltpu.SemaphoreType.DMA((CHUNKS + 1,)),
            pltpu.SemaphoreType.DMA((2,)),
            pltpu.SemaphoreType.DMA((2,)),
            pltpu.SemaphoreType.DMA((2,)),
            pltpu.SemaphoreType.DMA((2,)),
            pltpu.SemaphoreType.REGULAR((n_snap // 2,)),
            pltpu.SMEM((snap_dev, slot_total), jnp.int32),
            pltpu.SMEM((snap_dev, slot_total), jnp.int32),
            pltpu.SMEM((snap_dev,), jnp.int32),
        ],
        compiler_params=pltpu.CompilerParams(collective_id=0, has_side_effects=True),
    )(*operands[1:4], node_features.transpose(0, 2, 1), *operands[4:])
    result = jnp.transpose(result.reshape(vert_count, LANES))
    return result.reshape(snap_dev, feat_width, vert_count).transpose(0, 2, 1)


def dispatch(n_snap, n_feat, *operands):
    snap_dev, vert_count, feat_width = operands[0].shape
    slot_total = operands[4].shape[1]
    snaps = n_snap * snap_dev
    fits = (
        snap_dev == 2
        and 2 * feat_width == LANES
        and n_feat == 2 * snap_dev
        and n_snap >= 8
        and n_snap % 4 == 0
        and vert_count % (n_feat // snap_dev * snaps * SUBLANES) == 0
        and snaps * SUBLANES == LANES
        and vert_count >= 4 * SUBLANES * snaps
        and slot_total <= 16
        and vert_count <= 1024
    )
    if fits:
        return on_device_fused(n_snap, n_feat, *operands)
    return on_device(*operands)


def solution(mesh):
    placed = (
        P("snap", None, "feat"),
        P("snap", None),
        P("snap", None),
        P("snap"),
        P("snap", None, None, None),
        P(),
        P(),
        P(),
        P(),
        P(),
        P(),
    )
    return jax.shard_map(
        functools.partial(dispatch, mesh.shape["snap"], mesh.shape["feat"]), mesh=mesh, in_specs=placed, out_specs=P("snap", None, "feat"), check_vma=False
    )
```

```python
import functools
import math

import jax
import jax.numpy as jnp
from jax import lax
from jax.experimental import pallas as pl
from jax.experimental.pallas import tpu as pltpu
from jax.sharding import PartitionSpec as P

HEADS = 8


masked_score = -1e30


def spread_padded(features, tile_block, block_rows, block_cols, slot_count):
    vert_count, feat_width = features.shape
    tile_side = tile_block.shape[1]
    slot_total = tile_block.shape[0]
    block_count = vert_count // tile_side
    blocked = features.reshape(block_count, tile_side, feat_width)
    picked_blocks = blocked[block_cols]
    live_slots = jnp.arange(slot_total, dtype=jnp.int32) < slot_count
    products = jnp.einsum(
        "irc,icf->irf", tile_block, picked_blocks, preferred_element_type=jnp.float32
    )
    products = products * live_slots.astype(jnp.float32)[:, None, None]
    membership = (
        (block_rows[None, :] == jnp.arange(block_count, dtype=jnp.int32)[:, None])
        & live_slots[None, :]
    ).astype(jnp.float32)
    summed = jnp.dot(
        membership,
        products.reshape(slot_total, tile_side * feat_width),
        precision=lax.Precision.HIGHEST,
    )
    return summed.reshape(vert_count, feat_width).astype(jnp.bfloat16)


def attend_local(hidden, query_weight, key_weight, value_weight, out_weight):
    snaps, verts, model_width = hidden.shape
    head_dim = model_width // HEADS
    flat = hidden.reshape(snaps * verts, model_width)

    def project(weight):
        return (
            jnp.dot(flat, weight, preferred_element_type=jnp.float32)
            .astype(jnp.bfloat16)
            .reshape(snaps, verts, HEADS, head_dim)
        )

    query_heads = project(query_weight)
    key_heads = project(key_weight)
    value_heads = project(value_weight)
    scores = jnp.einsum(
        "tvhd,uvhd->vhtu", query_heads, key_heads, preferred_element_type=jnp.float32
    ) * head_dim ** (-0.5)
    causal = (
        jnp.arange(snaps, dtype=jnp.int32)[:, None] >= jnp.arange(snaps, dtype=jnp.int32)[None, :]
    )
    scores = jnp.where(causal, scores, masked_score)
    row_max = jnp.max(scores, axis=-1, keepdims=True)
    lifted = jnp.exp(scores - row_max)
    weights = (lifted / jnp.sum(lifted, axis=-1, keepdims=True)).astype(jnp.bfloat16)
    context = jnp.einsum(
        "vhtu,uvhd->tvhd", weights, value_heads, preferred_element_type=jnp.float32
    ).astype(jnp.bfloat16)
    context = context.reshape(snaps * verts, model_width)
    result = flat.astype(jnp.float32) + jnp.dot(
        context, out_weight, preferred_element_type=jnp.float32
    )
    return result.astype(jnp.bfloat16).reshape(snaps, verts, model_width)


def on_device(
    node_features,
    tile_rows,
    tile_cols,
    tile_counts,
    tile_values,
    layer_one,
    layer_two,
    query_weight,
    key_weight,
    value_weight,
    out_weight,
):
    snap_dev, vert_count, feat_width = node_features.shape
    feat_index = lax.axis_index("feat")

    def spread_all(features):
        spread_pieces = []
        for snapshot in range(snap_dev):
            spread_pieces.append(
                spread_padded(
                    features[snapshot],
                    tile_values[snapshot],
                    tile_rows[snapshot],
                    tile_cols[snapshot],
                    tile_counts[snapshot],
                )
            )
        return jnp.stack(spread_pieces, axis=0)

    def convolve(features, weight):
        spread_rows = spread_all(features).reshape(snap_dev * vert_count, feat_width)
        own_columns = lax.dynamic_slice_in_dim(weight, feat_index * feat_width, feat_width, 1)
        mixed_sum = jnp.dot(
            lax.all_gather(spread_rows, "feat", axis=1, tiled=True),
            own_columns,
            preferred_element_type=jnp.float32,
        )
        mixed_sum = mixed_sum.reshape(snap_dev, vert_count, feat_width)
        return (features.astype(jnp.float32) + jnp.maximum(mixed_sum, 0.0)).astype(jnp.bfloat16)

    hidden_one = convolve(node_features, layer_one)
    hidden_two = convolve(hidden_one, layer_two)
    vertex_rows = lax.all_to_all(
        lax.all_to_all(hidden_two, "snap", split_axis=1, concat_axis=0, tiled=True),
        "feat",
        split_axis=1,
        concat_axis=2,
        tiled=True,
    )
    attended = attend_local(vertex_rows, query_weight, key_weight, value_weight, out_weight)
    return lax.all_to_all(
        lax.all_to_all(attended, "feat", split_axis=2, concat_axis=1, tiled=True),
        "snap",
        split_axis=0,
        concat_axis=1,
        tiled=True,
    )


LANES = 128
CHUNKS = 2
LENT = (1, 2)
SUBLANES = 8
MESH = pl.DeviceIdType.MESH


def fused_kernel(
    n_snap,
    n_feat,
    rows_hbm,
    cols_hbm,
    counts_hbm,
    feat_ref,
    tiles_ref,
    w_one,
    w_two,
    w_query,
    w_key,
    w_value,
    w_out,
    returned,
    tiles,
    weights,
    away,
    pieces,
    adjacency,
    features,
    hidden_one,
    hidden_two,
    vertex_rows,
    outgoing,
    lending,
    load_sem,
    gather_send,
    gather_recv,
    spread_send,
    spread_recv,
    return_send,
    return_recv,
    heard,
    rows_ref,
    cols_ref,
    counts_ref,
):
    snap_dev, feat_width, vert_count = feat_ref.shape
    slot_total, tile_side, _ = tiles.shape
    block_count = vert_count // tile_side
    snaps, vert_dev, width = vertex_rows.shape
    half_snaps = snaps // 2
    parts = n_feat // snap_dev
    part_rows = vert_count // parts
    head_dim = width // HEADS

    me_snap = lax.axis_index("snap")
    me_feat = lax.axis_index("feat")
    part = me_feat % parts
    local = me_feat // parts
    own = me_snap * snap_dev + local
    half = own // half_snaps
    rank = own % half_snaps
    is_low = half == 0
    is_high = half == 1

    def load(source, target, at):
        copy = pltpu.make_async_copy(source, target, load_sem.at[at])
        copy.start()
        return copy

    def settle(ref, semaphore):
        pltpu.make_async_copy(ref, ref, semaphore).wait()

    barrier = pltpu.get_barrier_semaphore()
    plane = 2
    twin = me_snap + 1 - 2 * (me_snap % 2)
    mates = [(me_feat + step) % n_feat for step in range(1, n_feat)]
    has_below = me_snap >= plane
    has_above = me_snap < n_snap - plane
    column_count = has_below.astype(jnp.int32) + has_above.astype(jnp.int32)

    lead = local * parts + parts - 1

    def signal(semaphore, peer):
        pl.semaphore_signal(semaphore, inc=1, device_id=peer, device_id_type=MESH)

    def tell_column(semaphore):
        @pl.when(has_below)
        def _():
            signal(semaphore, (me_snap - plane, lead))

        @pl.when(has_above)
        def _():
            signal(semaphore, (me_snap + plane, lead))

    def tell_mates(semaphore):
        for mate in mates:
            signal(semaphore, (me_snap, mate))

    leads = part == parts - 1
    lead_count = leads.astype(jnp.int32)
    tell_mates(barrier)

    @pl.when(leads)
    def _():
        signal(barrier, (twin, me_feat))

    @pl.when(leads | (column_count == 1))
    def _():
        tell_column(barrier)

    level = me_snap // plane
    near_end = (level == 1).astype(jnp.int32) + (level == n_snap // plane - 2).astype(jnp.int32)
    partner = (me_feat + parts) % n_feat
    away_load = load(feat_ref.at[partner // parts], away, 6)
    own_load = load(feat_ref.at[local], pieces.at[me_feat], 0)
    list_loads = [
        load(ref, kept, 2 + at)
        for at, (ref, kept) in enumerate(
            ((rows_hbm, rows_ref), (cols_hbm, cols_ref), (counts_hbm, counts_ref))
        )
    ]
    tile_load = load(tiles_ref.at[local], tiles, 1)
    weight_list = (w_one, w_two, w_query, w_key, w_value, w_out)
    pl.semaphore_wait(barrier, len(mates) + lead_count * (1 + column_count + near_end))

    mate = local * parts + 1 - part
    across = (partner // parts) * parts + 1 - part
    chunk = feat_width // CHUNKS
    spans = [pl.ds(at * chunk, chunk) for at in range(CHUNKS)]
    whole = pl.ds(0, feat_width)

    def gather(source, span, at, peer):
        pltpu.make_async_remote_copy(
            src_ref=source.at[span],
            dst_ref=pieces.at[me_feat, span],
            send_sem=gather_send,
            recv_sem=gather_recv.at[at],
            device_id=(me_snap, peer),
            device_id_type=MESH,
        ).start()

    own_load.wait()
    gather(pieces.at[me_feat], whole, CHUNKS, mate)
    away_load.wait()

    @pl.when(leads)
    def _():
        for at in range(CHUNKS):
            gather(away, spans[at], at, partner)

    @pl.when(part == 0)
    def _():
        gather(away, whole, CHUNKS, partner)
        gather(away, whole, CHUNKS, across)


    def relay(at):
        passed = pieces.at[partner, spans[at]]
        settle(passed, gather_recv.at[at])
        pltpu.make_async_remote_copy(
            src_ref=passed,
            dst_ref=passed,
            send_sem=gather_send,
            recv_sem=gather_recv.at[CHUNKS],
            device_id=(me_snap, mate),
            device_id_type=MESH,
        ).start()

    for at, ref in enumerate(weight_list):
        load(ref, weights.at[at], 5)

    hops = n_snap // plane - 2

    @pl.when(leads)
    def _():
        tell_column(heard.at[0])

    tile_load.wait()
    for copy in list_loads:
        copy.wait()
    slot_count = counts_ref[local]
    strip = 2 * SUBLANES
    places = []
    for slot in range(slot_total):
        place = rows_ref[local, slot] * block_count + cols_ref[local, slot]
        place = jnp.where(slot < slot_count, place, -1)
        places.append(jnp.full((strip, tile_side), place, jnp.int32))

    def build(at, carry):
        first = pl.multiple_of(at * strip, strip)
        listed = [
            tiles[slot, pl.ds(first, strip), :].astype(jnp.float32) for slot in range(slot_total)
        ]
        for row in range(block_count):
            for col in range(block_count):
                summed = jnp.zeros((strip, tile_side), jnp.float32)
                for slot in range(slot_total):
                    summed += jnp.where(
                        places[slot] == row * block_count + col, listed[slot], 0.0
                    )
                start = pl.multiple_of(row * tile_side + first, strip)
                adjacency[pl.ds(start, strip), col * tile_side : (col + 1) * tile_side] = (
                    summed.astype(jnp.bfloat16)
                )
        return carry

    strips = tile_side // strip
    lax.fori_loop(0, strips // 2, build, 0)
    lax.fori_loop(strips // 2, strips, build, 0)
    for hop in range(hops - 1):

        @pl.when(leads)
        def _():
            pl.semaphore_wait(heard.at[hop], column_count)
            tell_column(heard.at[hop + 1])


    @pl.when(leads)
    def _():
        pl.semaphore_wait(heard.at[hops - 1], column_count)
        signal(heard.at[hops], (twin, me_feat))

    @pl.when(leads)
    def _():
        for at in range(CHUNKS):
            relay(at)
        pl.semaphore_wait(heard.at[hops], 1)
        tell_mates(heard.at[hops + 1])


    settle(weights, load_sem.at[5])

    @pl.when(leads)
    def _():
        settle(pieces.at[pl.ds(0, n_feat - 2)], gather_recv.at[CHUNKS])

    @pl.when(part == 0)
    def _():
        settle(pieces.at[pl.ds(0, n_feat - 1)], gather_recv.at[CHUNKS])

    def mix(lhs, source, before, weight, turned=None):
        if turned is None:
            spread = jnp.dot(lhs, source, preferred_element_type=jnp.float32)
        else:
            spread = lax.dot_general(
                lhs, turned, (((1,), (1,)), ((), ())), preferred_element_type=jnp.float32
            )
        mixed = jnp.dot(
            spread.astype(jnp.bfloat16), weight, preferred_element_type=jnp.float32
        )
        return (before.astype(jnp.float32) + jnp.maximum(mixed, 0.0)).astype(jnp.bfloat16)

    side = half_snaps // 2
    far = rank // side
    keeps = [vert_dev - each * SUBLANES for each in LENT]
    lends = [each * SUBLANES for each in LENT]
    kept_rows = [pl.ds(0, each) for each in keeps]
    lent_rows = [pl.ds(keep, lend) for keep, lend in zip(keeps, lends)]
    all_rows = pl.ds(0, vert_dev)

    def spread_to(target_half, peer, rows):
        target = target_half * half_snaps + peer
        pltpu.make_async_remote_copy(
            src_ref=hidden_two.at[peer, rows],
            dst_ref=vertex_rows.at[own, rows],
            send_sem=spread_send.at[target_half],
            recv_sem=spread_recv.at[half],
            device_id=(target // snap_dev, (target % snap_dev) * parts + part),
            device_id_type=MESH,
        ).start()

    def flip(index, mask):
        flipped = 0
        for bit in (4, 2, 1):
            digit = index // bit % 2
            flipped = flipped + bit * (1 - digit if mask & bit else digit)
        return flipped

    def spread_half(target_half, rows):
        for mask in (7, 6, 5, 3, 4, 2, 1):
            spread_to(target_half, flip(rank, mask), rows)

    near = rank % (half_snaps // 2)
    own_rows = pl.ds(pl.multiple_of(part * part_rows, part_rows), part_rows)
    turned = pieces[...].reshape(width, vert_count)
    block = vert_count // 1
    spread_two = jnp.zeros((part_rows, width), jnp.float32)
    for first in range(0, vert_count, block):
        before = jnp.transpose(turned[:, first : first + block])
        hidden = mix(adjacency[first : first + block, :], None, before, weights[0], turned)
        hidden_one[first : first + block, :] = hidden
        spread_two += jnp.dot(
            adjacency[own_rows, first : first + block],
            hidden,
            preferred_element_type=jnp.float32,
        )
    mixed_two = jnp.dot(
        spread_two.astype(jnp.bfloat16), weights[1], preferred_element_type=jnp.float32
    )
    hidden_two[...] = (
        (hidden_one[own_rows, :].astype(jnp.float32) + jnp.maximum(mixed_two, 0.0))
        .astype(jnp.bfloat16)
        .reshape(half_snaps, vert_dev, width)
    )
    pl.semaphore_wait(heard.at[hops + 1], snap_dev - lead_count)

    @pl.when(is_low)
    def _():
        spread_half(0, all_rows)
        for high in (1, 0):
            for mask in (3, 2, 1, 0):
                spread_to(1, high * side + flip(near, mask), kept_rows[high])
    @pl.when(is_high)
    def _():
        for high in (0, 1):
            for mask in (3, 2, 1, 0):
                spread_to(0, high * side + flip(near, mask), lent_rows[high])

    for high in range(2):

        @pl.when(is_high & (far == high))
        def _():
            for mask in (7, 6, 5, 3, 4, 2, 1):
                peer_high = high if mask < 4 else 1 - high
                spread_to(
                    1, peer_high * side + flip(near, mask % 4), kept_rows[peer_high]
                )


    vertex_rows[own] = hidden_two[rank]

    groups = vert_dev // SUBLANES
    group_rows = half_snaps * SUBLANES
    pair = 2 * group_rows
    pair_dims = 2 * head_dim
    quads = width // LANES
    quad_pairs = LANES // pair_dims
    half_dev = n_snap // 2

    def split(array):
        array = array.reshape(half_snaps, -1, SUBLANES, width)
        return [array[:, at].reshape(group_rows, width) for at in range(array.shape[1])]

    def project(flat, at):
        return split(jnp.dot(flat, weights[at], preferred_element_type=jnp.float32))

    def score(keys, turned):
        keys = keys.astype(jnp.bfloat16)
        return [
            jnp.dot(
                keys[:, at * LANES : (at + 1) * LANES],
                turned[at],
                preferred_element_type=jnp.float32,
            )
            for at in range(quads)
        ]

    quad_columns = quad_pairs * pair
    row_at = lax.broadcasted_iota(jnp.int32, (group_rows, quad_columns), 0)
    col_at = lax.broadcasted_iota(jnp.int32, (group_rows, quad_columns), 1) % group_rows
    same = row_at % SUBLANES == col_at % SUBLANES
    visible = same & (row_at // SUBLANES <= col_at // SUBLANES)
    factor = head_dim ** (-0.5) * math.log2(math.e)
    none = jnp.zeros((pair_dims, pair), jnp.bfloat16)
    ones = jnp.ones((2 * SUBLANES, group_rows), jnp.bfloat16)

    def masked(keys, queries, seen):
        return [jnp.where(seen, each, masked_score) for each in score(keys, queries)]

    def turn(listed):
        doubled = jnp.concatenate([query for query in listed for _ in range(2)], axis=0)
        turned = jnp.transpose(doubled.astype(jnp.bfloat16))
        turned_head = lax.broadcasted_iota(jnp.int32, turned.shape, 0) // head_dim
        turned_side = lax.broadcasted_iota(jnp.int32, turned.shape, 1) // group_rows
        turned = jnp.where(turned_head % 2 == turned_side % 2, turned, 0.0)
        queries = []
        for at in range(len(listed)):
            columns = turned[:, at * pair : (at + 1) * pair]
            pairs = [
                columns[first : first + pair_dims] for first in range(0, width, pair_dims)
            ]
            queries.append(
                [
                    jnp.concatenate(
                        [
                            jnp.concatenate(
                                [
                                    pairs[quad * quad_pairs + inner] if inner == outer else none
                                    for inner in range(quad_pairs)
                                ],
                                axis=0,
                            )
                            for outer in range(quad_pairs)
                        ],
                        axis=1,
                    )
                    for quad in range(quads)
                ]
            )
        return queries

    def attend(scores_of, values_of, before):
        lane_odd = lax.broadcasted_iota(jnp.int32, (group_rows, width), 1) // head_dim % 2 == 1
        count = len(before)
        contexts = []
        for at in range(count):
            value = jnp.transpose(
                jnp.concatenate([each[at] for each in values_of], axis=0).astype(jnp.bfloat16)
            )
            tail = jnp.concatenate([ones] * len(values_of), axis=1)
            context = []
            for quad in range(quads):
                listed = [each[at][quad] for each in scores_of]
                highest = functools.reduce(
                    jnp.maximum, [jnp.max(each, axis=0, keepdims=True) for each in listed]
                )
                shares = jnp.concatenate(
                    [
                        jnp.exp2((each - highest) * factor).astype(jnp.bfloat16)
                        for each in listed
                    ],
                    axis=0,
                )
                for inner in range(quad_pairs):
                    first = (quad * quad_pairs + inner) * pair_dims
                    product = jnp.dot(
                        jnp.concatenate([value[first : first + pair_dims], tail], axis=0),
                        shares[:, inner * pair : (inner + 1) * pair],
                        preferred_element_type=jnp.float32,
                    )
                    scale = 1.0 / product[pair_dims : pair_dims + 1]
                    context.append((product[:pair_dims] * scale).astype(jnp.bfloat16))
            context = jnp.transpose(jnp.concatenate(context, axis=0))
            contexts.append(jnp.where(lane_odd, context[group_rows:], context[:group_rows]))
        mixed = jnp.dot(
            jnp.concatenate(contexts, axis=0), weights[5], preferred_element_type=jnp.float32
        ).reshape(count, group_rows, width)
        verts = count * SUBLANES
        evolved = jnp.concatenate(
            [
                (before[at] + mixed[at]).reshape(half_snaps, 1, SUBLANES, width)
                for at in range(count)
            ],
            axis=1,
        ).reshape(half_dev, snap_dev, verts, width)
        low = lax.broadcasted_iota(jnp.int32, (half_dev * verts, LANES), 1) < feat_width
        outs = []
        for at in range(0, n_feat, 2):
            lanes = slice(at * feat_width, (at + 2) * feat_width)
            first = evolved[:, 0, :, lanes].reshape(half_dev * verts, LANES)
            second = evolved[:, 1, :, lanes].reshape(half_dev * verts, LANES)
            even = jnp.where(low, first, pltpu.roll(second, feat_width, 1))
            odd = jnp.where(low, pltpu.roll(first, feat_width, 1), second)
            outs += [each.reshape(half_dev, verts, LANES) for each in (even, odd)]
        return outs

    total = half_dev * n_feat
    outgoing_rows = outgoing.reshape(total * vert_dev, LANES)
    me = (me_snap % half_dev) * n_feat + me_feat

    def hand_back(source, target_half, peer, rows, source_rows, at):
        pltpu.make_async_remote_copy(
            src_ref=source.at[peer % n_feat, peer // n_feat, source_rows],
            dst_ref=returned.at[part, rank, rows],
            send_sem=return_send.at[at],
            recv_sem=return_recv.at[at],
            device_id=(target_half * half_dev + peer // n_feat, peer % n_feat),
            device_id_type=MESH,
        ).start()

    masks = (14, 15, 12, 13, 10, 11, 6, 7, 8, 9, 4, 5, 2, 3, 1, 0)
    mirrored = [
        flip(me // 2, mask // 2) * 2 + (1 - me % 2 if mask % 2 else me % 2) for mask in masks
    ]

    def own_part(rows):
        flat = rows.reshape(half_snaps * vert_dev, width)
        return project(flat, 2), project(flat, 3), project(flat, 4), split(flat.astype(jnp.float32))

    @pl.when(is_low)
    def _():
        settle(vertex_rows.at[pl.ds(0, half_snaps - 1)], spread_recv.at[0])
        queries, keys, values, before = own_part(vertex_rows[pl.ds(0, half_snaps)])
        queries = turn(queries)
        scores = [masked(keys[at], queries[at], visible) for at in range(groups)]
        for at, out in enumerate(attend([scores], [values], before)):
            outgoing[at] = out.astype(jnp.bfloat16)
        for peer in mirrored[:-1]:
            hand_back(outgoing, 0, peer, all_rows, all_rows, 0)
        load(outgoing.at[me_feat, me_snap % half_dev], returned.at[part, rank], 0)
        for high in range(2):

            @pl.when(far == high)
            def _():
                count = LENT[high]
                settle(
                    vertex_rows.at[pl.ds(0, half_snaps), lent_rows[high]], spread_recv.at[1]
                )
                base = keeps[high] // (2 * SUBLANES) * 2 * SUBLANES
                lent = vertex_rows[
                    pl.ds(half_snaps, half_snaps), pl.ds(base, vert_dev - base)
                ].astype(jnp.float32)[:, keeps[high] - base :]
                flats = split(lent)
                rounded = jnp.concatenate(flats, axis=0).astype(jnp.bfloat16)

                def lent_part(at):
                    out = jnp.dot(rounded, weights[at], preferred_element_type=jnp.float32)
                    return [
                        out[each * group_rows : (each + 1) * group_rows]
                        for each in range(count)
                    ]

                turned = turn(lent_part(2))
                lent_keys = lent_part(3)
                scores = [masked(lent_keys[at], turned[at], visible) for at in range(count)]
                scores_low = [
                    masked(keys[groups - count + at], turned[at], same)
                    for at in range(count)
                ]
                outs = attend(
                    [scores_low, scores], [values[groups - count :], lent_part(4)], flats
                )
                for at, out in enumerate(outs):
                    lending[at, :, pl.ds(0, lends[high])] = out.astype(jnp.bfloat16)
                for peer in mirrored:
                    hand_back(lending, 1, peer, lent_rows[high], pl.ds(0, lends[high]), 1)
                settle(outgoing_rows.at[pl.ds(0, total * lends[high])], return_send.at[1])

        settle(hidden_one.at[pl.ds(0, side * sum(keeps))], spread_send.at[1])
        settle(hidden_two.at[pl.ds(0, half_snaps - 1)], spread_send.at[0])
        pltpu.make_async_copy(
            outgoing.at[0, 0], returned.at[part, rank], load_sem.at[0]
        ).wait()
        everyone = outgoing_rows.at[pl.ds(0, (total - 1) * vert_dev)]
        settle(everyone, return_recv.at[0])
        settle(everyone, return_send.at[0])

    for high in range(2):

        @pl.when(is_high & (far == high))
        def _():
            keep = keeps[high]
            count = groups - LENT[high]
            kept = kept_rows[high]
            settle(vertex_rows.at[pl.ds(0, half_snaps - 1), kept], spread_recv.at[1])
            queries, keys, values, before = own_part(
                vertex_rows[pl.ds(half_snaps, half_snaps)]
            )
            queries = turn(queries[:count])
            scores = [masked(keys[at], queries[at], visible) for at in range(count)]
            settle(vertex_rows.at[pl.ds(0, half_snaps), kept], spread_recv.at[0])
            flat_low = vertex_rows[pl.ds(0, half_snaps)].reshape(half_snaps * vert_dev, width)
            keys_low, values_low = project(flat_low, 3), project(flat_low, 4)
            scores_low = [masked(keys_low[at], queries[at], same) for at in range(count)]
            outs = attend([scores_low, scores], [values_low, values], before[:count])
            for at, out in enumerate(outs):
                outgoing[at, :, kept] = out.astype(jnp.bfloat16)
            for peer in mirrored[:-1]:
                hand_back(outgoing, 1, peer, kept, kept, 0)
            own_copy = load(
                outgoing.at[me_feat, me_snap % half_dev, kept], returned.at[part, rank, kept], 0
            )
            settle(hidden_one.at[pl.ds(0, side * sum(lends))], spread_send.at[0])
            settle(
                hidden_one.at[pl.ds(0, side * sum(keeps) - keep)], spread_send.at[1]
            )
            own_copy.wait()
            settle(
                outgoing_rows.at[pl.ds(0, total // 2 * sum(keeps) - keep)], return_recv.at[0]
            )
            settle(
                outgoing_rows.at[pl.ds(0, total // 2 * sum(lends))], return_recv.at[1]
            )
            settle(outgoing_rows.at[pl.ds(0, (total - 1) * keep)], return_send.at[0])

    settle(pieces.at[pl.ds(0, n_feat - 1)], gather_send)


def on_device_fused(n_snap, n_feat, *operands):
    node_features, _, _, _, tile_values, layer_one = operands[:6]
    snap_dev, vert_count, feat_width = node_features.shape
    _, slot_total, tile_side, _ = tile_values.shape
    width = layer_one.shape[0]
    parts = n_feat // snap_dev
    snaps = n_snap * snap_dev
    half_snaps = snaps // 2
    vert_dev = vert_count // (parts * half_snaps)
    kept = jnp.bfloat16
    result = pl.pallas_call(
        functools.partial(fused_kernel, n_snap, n_feat),
        out_shape=pltpu.VMEM((parts, half_snaps, vert_dev, LANES), kept),
        in_specs=[pl.BlockSpec(memory_space=pltpu.HBM)] * 11,
        out_specs=pl.BlockSpec(memory_space=pltpu.VMEM),
        scratch_shapes=[
            pltpu.VMEM((slot_total, tile_side, tile_side), kept),
            pltpu.VMEM((6, width, width), kept),
            pltpu.VMEM((feat_width, vert_count), kept),
            pltpu.VMEM((n_feat, feat_width, vert_count), kept),
            pltpu.VMEM((vert_count, vert_count), kept),
            pltpu.VMEM((vert_count, width), kept),
            pltpu.VMEM((vert_count, width), kept),
            pltpu.VMEM((half_snaps, vert_dev, width), kept),
            pltpu.VMEM((snaps, vert_dev, width), kept),
            pltpu.VMEM((n_feat, n_snap // 2, vert_dev, LANES), kept),
            pltpu.VMEM((n_feat, n_snap // 2, max(LENT) * SUBLANES, LANES), kept),
            pltpu.SemaphoreType.DMA((7,)),
            pltpu.SemaphoreType.DMA,
            pltpu.SemaphoreType.DMA((CHUNKS + 1,)),
            pltpu.SemaphoreType.DMA((2,)),
            pltpu.SemaphoreType.DMA((2,)),
            pltpu.SemaphoreType.DMA((2,)),
            pltpu.SemaphoreType.DMA((2,)),
            pltpu.SemaphoreType.REGULAR((n_snap // 2,)),
            pltpu.SMEM((snap_dev, slot_total), jnp.int32),
            pltpu.SMEM((snap_dev, slot_total), jnp.int32),
            pltpu.SMEM((snap_dev,), jnp.int32),
        ],
        compiler_params=pltpu.CompilerParams(collective_id=0, has_side_effects=True),
    )(*operands[1:4], node_features.transpose(0, 2, 1), *operands[4:])
    result = jnp.transpose(result.reshape(vert_count, LANES))
    return result.reshape(snap_dev, feat_width, vert_count).transpose(0, 2, 1)


def dispatch(n_snap, n_feat, *operands):
    snap_dev, vert_count, feat_width = operands[0].shape
    slot_total = operands[4].shape[1]
    snaps = n_snap * snap_dev
    fits = (
        snap_dev == 2
        and 2 * feat_width == LANES
        and n_feat == 2 * snap_dev
        and n_snap >= 8
        and n_snap % 4 == 0
        and vert_count % (n_feat // snap_dev * snaps * SUBLANES) == 0
        and snaps * SUBLANES == LANES
        and vert_count >= 4 * SUBLANES * snaps
        and slot_total <= 16
        and vert_count <= 1024
    )
    if fits:
        return on_device_fused(n_snap, n_feat, *operands)
    return on_device(*operands)


def solution(mesh):
    placed = (
        P("snap", None, "feat"),
        P("snap", None),
        P("snap", None),
        P("snap"),
        P("snap", None, None, None),
        P(),
        P(),
        P(),
        P(),
        P(),
        P(),
    )
    return jax.shard_map(
        functools.partial(dispatch, mesh.shape["snap"], mesh.shape["feat"]), mesh=mesh, in_specs=placed, out_specs=P("snap", None, "feat"), check_vma=False
    )
```

```python
import functools
import math

import jax
import jax.numpy as jnp
from jax import lax
from jax.experimental import pallas as pl
from jax.experimental.pallas import tpu as pltpu
from jax.sharding import PartitionSpec as P

HEADS = 8


masked_score = -1e30


def spread_padded(features, tile_block, block_rows, block_cols, slot_count):
    vert_count, feat_width = features.shape
    tile_side = tile_block.shape[1]
    slot_total = tile_block.shape[0]
    block_count = vert_count // tile_side
    blocked = features.reshape(block_count, tile_side, feat_width)
    picked_blocks = blocked[block_cols]
    live_slots = jnp.arange(slot_total, dtype=jnp.int32) < slot_count
    products = jnp.einsum(
        "irc,icf->irf", tile_block, picked_blocks, preferred_element_type=jnp.float32
    )
    products = products * live_slots.astype(jnp.float32)[:, None, None]
    membership = (
        (block_rows[None, :] == jnp.arange(block_count, dtype=jnp.int32)[:, None])
        & live_slots[None, :]
    ).astype(jnp.float32)
    summed = jnp.dot(
        membership,
        products.reshape(slot_total, tile_side * feat_width),
        precision=lax.Precision.HIGHEST,
    )
    return summed.reshape(vert_count, feat_width).astype(jnp.bfloat16)


def attend_local(hidden, query_weight, key_weight, value_weight, out_weight):
    snaps, verts, model_width = hidden.shape
    head_dim = model_width // HEADS
    flat = hidden.reshape(snaps * verts, model_width)

    def project(weight):
        return (
            jnp.dot(flat, weight, preferred_element_type=jnp.float32)
            .astype(jnp.bfloat16)
            .reshape(snaps, verts, HEADS, head_dim)
        )

    query_heads = project(query_weight)
    key_heads = project(key_weight)
    value_heads = project(value_weight)
    scores = jnp.einsum(
        "tvhd,uvhd->vhtu", query_heads, key_heads, preferred_element_type=jnp.float32
    ) * head_dim ** (-0.5)
    causal = (
        jnp.arange(snaps, dtype=jnp.int32)[:, None] >= jnp.arange(snaps, dtype=jnp.int32)[None, :]
    )
    scores = jnp.where(causal, scores, masked_score)
    row_max = jnp.max(scores, axis=-1, keepdims=True)
    lifted = jnp.exp(scores - row_max)
    weights = (lifted / jnp.sum(lifted, axis=-1, keepdims=True)).astype(jnp.bfloat16)
    context = jnp.einsum(
        "vhtu,uvhd->tvhd", weights, value_heads, preferred_element_type=jnp.float32
    ).astype(jnp.bfloat16)
    context = context.reshape(snaps * verts, model_width)
    result = flat.astype(jnp.float32) + jnp.dot(
        context, out_weight, preferred_element_type=jnp.float32
    )
    return result.astype(jnp.bfloat16).reshape(snaps, verts, model_width)


def on_device(
    node_features,
    tile_rows,
    tile_cols,
    tile_counts,
    tile_values,
    layer_one,
    layer_two,
    query_weight,
    key_weight,
    value_weight,
    out_weight,
):
    snap_dev, vert_count, feat_width = node_features.shape
    feat_index = lax.axis_index("feat")

    def spread_all(features):
        spread_pieces = []
        for snapshot in range(snap_dev):
            spread_pieces.append(
                spread_padded(
                    features[snapshot],
                    tile_values[snapshot],
                    tile_rows[snapshot],
                    tile_cols[snapshot],
                    tile_counts[snapshot],
                )
            )
        return jnp.stack(spread_pieces, axis=0)

    def convolve(features, weight):
        spread_rows = spread_all(features).reshape(snap_dev * vert_count, feat_width)
        own_columns = lax.dynamic_slice_in_dim(weight, feat_index * feat_width, feat_width, 1)
        mixed_sum = jnp.dot(
            lax.all_gather(spread_rows, "feat", axis=1, tiled=True),
            own_columns,
            preferred_element_type=jnp.float32,
        )
        mixed_sum = mixed_sum.reshape(snap_dev, vert_count, feat_width)
        return (features.astype(jnp.float32) + jnp.maximum(mixed_sum, 0.0)).astype(jnp.bfloat16)

    hidden_one = convolve(node_features, layer_one)
    hidden_two = convolve(hidden_one, layer_two)
    vertex_rows = lax.all_to_all(
        lax.all_to_all(hidden_two, "snap", split_axis=1, concat_axis=0, tiled=True),
        "feat",
        split_axis=1,
        concat_axis=2,
        tiled=True,
    )
    attended = attend_local(vertex_rows, query_weight, key_weight, value_weight, out_weight)
    return lax.all_to_all(
        lax.all_to_all(attended, "feat", split_axis=2, concat_axis=1, tiled=True),
        "snap",
        split_axis=0,
        concat_axis=1,
        tiled=True,
    )


LANES = 128
CHUNKS = 2
LENT = (1, 2)
SUBLANES = 8
MESH = pl.DeviceIdType.MESH


def fused_kernel(
    n_snap,
    n_feat,
    rows_hbm,
    cols_hbm,
    counts_hbm,
    feat_ref,
    tiles_ref,
    w_one,
    w_two,
    w_query,
    w_key,
    w_value,
    w_out,
    returned,
    tiles,
    weights,
    away,
    pieces,
    adjacency,
    features,
    hidden_one,
    hidden_two,
    vertex_rows,
    outgoing,
    lending,
    load_sem,
    gather_send,
    gather_recv,
    spread_send,
    spread_recv,
    return_send,
    return_recv,
    heard,
    rows_ref,
    cols_ref,
    counts_ref,
):
    snap_dev, feat_width, vert_count = feat_ref.shape
    slot_total, tile_side, _ = tiles.shape
    block_count = vert_count // tile_side
    snaps, vert_dev, width = vertex_rows.shape
    half_snaps = snaps // 2
    parts = n_feat // snap_dev
    part_rows = vert_count // parts
    head_dim = width // HEADS

    me_snap = lax.axis_index("snap")
    me_feat = lax.axis_index("feat")
    part = me_feat % parts
    local = me_feat // parts
    own = me_snap * snap_dev + local
    half = own // half_snaps
    rank = own % half_snaps
    is_low = half == 0
    is_high = half == 1

    def load(source, target, at):
        copy = pltpu.make_async_copy(source, target, load_sem.at[at])
        copy.start()
        return copy

    def settle(ref, semaphore):
        pltpu.make_async_copy(ref, ref, semaphore).wait()

    barrier = pltpu.get_barrier_semaphore()
    plane = 2
    twin = me_snap + 1 - 2 * (me_snap % 2)
    mates = [(me_feat + step) % n_feat for step in range(1, n_feat)]
    has_below = me_snap >= plane
    has_above = me_snap < n_snap - plane
    column_count = has_below.astype(jnp.int32) + has_above.astype(jnp.int32)

    lead = local * parts + parts - 1

    def signal(semaphore, peer):
        pl.semaphore_signal(semaphore, inc=1, device_id=peer, device_id_type=MESH)

    def tell_column(semaphore):
        @pl.when(has_below)
        def _():
            signal(semaphore, (me_snap - plane, lead))

        @pl.when(has_above)
        def _():
            signal(semaphore, (me_snap + plane, lead))

    def tell_mates(semaphore):
        for mate in mates:
            signal(semaphore, (me_snap, mate))

    leads = part == parts - 1
    lead_count = leads.astype(jnp.int32)
    tell_mates(barrier)

    @pl.when(leads)
    def _():
        signal(barrier, (twin, me_feat))

    @pl.when(leads | (column_count == 1))
    def _():
        tell_column(barrier)

    level = me_snap // plane
    near_end = (level == 1).astype(jnp.int32) + (level == n_snap // plane - 2).astype(jnp.int32)
    partner = (me_feat + parts) % n_feat
    away_load = load(feat_ref.at[partner // parts], away, 6)
    own_load = load(feat_ref.at[local], pieces.at[me_feat], 0)
    list_loads = [
        load(ref, kept, 2 + at)
        for at, (ref, kept) in enumerate(
            ((rows_hbm, rows_ref), (cols_hbm, cols_ref), (counts_hbm, counts_ref))
        )
    ]
    tile_load = load(tiles_ref.at[local], tiles, 1)
    weight_list = (w_one, w_two, w_query, w_key, w_value, w_out)
    pl.semaphore_wait(barrier, len(mates) + lead_count * (1 + column_count + near_end))

    mate = local * parts + 1 - part
    across = (partner // parts) * parts + 1 - part
    chunk = feat_width // CHUNKS
    spans = [pl.ds(at * chunk, chunk) for at in range(CHUNKS)]
    whole = pl.ds(0, feat_width)

    def gather(source, span, at, peer):
        pltpu.make_async_remote_copy(
            src_ref=source.at[span],
            dst_ref=pieces.at[me_feat, span],
            send_sem=gather_send,
            recv_sem=gather_recv.at[at],
            device_id=(me_snap, peer),
            device_id_type=MESH,
        ).start()

    own_load.wait()
    gather(pieces.at[me_feat], whole, CHUNKS, mate)
    away_load.wait()

    @pl.when(leads)
    def _():
        for at in range(CHUNKS):
            gather(away, spans[at], at, partner)

    @pl.when(part == 0)
    def _():
        gather(away, whole, CHUNKS, partner)
        gather(away, whole, CHUNKS, across)


    def relay(at):
        passed = pieces.at[partner, spans[at]]
        settle(passed, gather_recv.at[at])
        pltpu.make_async_remote_copy(
            src_ref=passed,
            dst_ref=passed,
            send_sem=gather_send,
            recv_sem=gather_recv.at[CHUNKS],
            device_id=(me_snap, mate),
            device_id_type=MESH,
        ).start()

    for at, ref in enumerate(weight_list):
        load(ref, weights.at[at], 5)

    hops = n_snap // plane - 2

    @pl.when(leads)
    def _():
        tell_column(heard.at[0])

    tile_load.wait()
    for copy in list_loads:
        copy.wait()
    slot_count = counts_ref[local]
    strip = 2 * SUBLANES
    places = []
    for slot in range(slot_total):
        place = rows_ref[local, slot] * block_count + cols_ref[local, slot]
        place = jnp.where(slot < slot_count, place, -1)
        places.append(jnp.full((strip, tile_side), place, jnp.int32))

    def build(at, carry):
        first = pl.multiple_of(at * strip, strip)
        listed = [
            tiles[slot, pl.ds(first, strip), :].astype(jnp.float32) for slot in range(slot_total)
        ]
        for row in range(block_count):
            for col in range(block_count):
                summed = jnp.zeros((strip, tile_side), jnp.float32)
                for slot in range(slot_total):
                    summed += jnp.where(
                        places[slot] == row * block_count + col, listed[slot], 0.0
                    )
                start = pl.multiple_of(row * tile_side + first, strip)
                adjacency[pl.ds(start, strip), col * tile_side : (col + 1) * tile_side] = (
                    summed.astype(jnp.bfloat16)
                )
        return carry

    strips = tile_side // strip
    lax.fori_loop(0, strips // 2, build, 0)
    lax.fori_loop(strips // 2, strips, build, 0)
    for hop in range(hops - 1):

        @pl.when(leads)
        def _():
            pl.semaphore_wait(heard.at[hop], column_count)
            tell_column(heard.at[hop + 1])


    @pl.when(leads)
    def _():
        pl.semaphore_wait(heard.at[hops - 1], column_count)
        signal(heard.at[hops], (twin, me_feat))

    @pl.when(leads)
    def _():
        for at in range(CHUNKS):
            relay(at)
        pl.semaphore_wait(heard.at[hops], 1)
        tell_mates(heard.at[hops + 1])


    settle(weights, load_sem.at[5])

    @pl.when(leads)
    def _():
        settle(pieces.at[pl.ds(0, n_feat - 2)], gather_recv.at[CHUNKS])

    @pl.when(part == 0)
    def _():
        settle(pieces.at[pl.ds(0, n_feat - 1)], gather_recv.at[CHUNKS])

    def mix(lhs, source, before, weight, turned=None):
        if turned is None:
            spread = jnp.dot(lhs, source, preferred_element_type=jnp.float32)
        else:
            spread = lax.dot_general(
                lhs, turned, (((1,), (1,)), ((), ())), preferred_element_type=jnp.float32
            )
        mixed = jnp.dot(
            spread.astype(jnp.bfloat16), weight, preferred_element_type=jnp.float32
        )
        return (before.astype(jnp.float32) + jnp.maximum(mixed, 0.0)).astype(jnp.bfloat16)

    side = half_snaps // 2
    far = rank // side
    keeps = [vert_dev - each * SUBLANES for each in LENT]
    lends = [each * SUBLANES for each in LENT]
    kept_rows = [pl.ds(0, each) for each in keeps]
    lent_rows = [pl.ds(keep, lend) for keep, lend in zip(keeps, lends)]
    all_rows = pl.ds(0, vert_dev)

    def spread_to(target_half, peer, rows):
        target = target_half * half_snaps + peer
        pltpu.make_async_remote_copy(
            src_ref=hidden_two.at[peer, rows],
            dst_ref=vertex_rows.at[own, rows],
            send_sem=spread_send.at[target_half],
            recv_sem=spread_recv.at[half],
            device_id=(target // snap_dev, (target % snap_dev) * parts + part),
            device_id_type=MESH,
        ).start()

    def flip(index, mask):
        flipped = 0
        for bit in (4, 2, 1):
            digit = index // bit % 2
            flipped = flipped + bit * (1 - digit if mask & bit else digit)
        return flipped

    def spread_half(target_half, rows):
        for mask in (7, 3, 6, 5, 2, 1, 4):
            spread_to(target_half, flip(rank, mask), rows)

    near = rank % (half_snaps // 2)
    own_rows = pl.ds(pl.multiple_of(part * part_rows, part_rows), part_rows)
    turned = pieces[...].reshape(width, vert_count)
    block = vert_count // 1
    spread_two = jnp.zeros((part_rows, width), jnp.float32)
    for first in range(0, vert_count, block):
        before = jnp.transpose(turned[:, first : first + block])
        hidden = mix(adjacency[first : first + block, :], None, before, weights[0], turned)
        hidden_one[first : first + block, :] = hidden
        spread_two += jnp.dot(
            adjacency[own_rows, first : first + block],
            hidden,
            preferred_element_type=jnp.float32,
        )
    mixed_two = jnp.dot(
        spread_two.astype(jnp.bfloat16), weights[1], preferred_element_type=jnp.float32
    )
    hidden_two[...] = (
        (hidden_one[own_rows, :].astype(jnp.float32) + jnp.maximum(mixed_two, 0.0))
        .astype(jnp.bfloat16)
        .reshape(half_snaps, vert_dev, width)
    )
    pl.semaphore_wait(heard.at[hops + 1], snap_dev - lead_count)

    @pl.when(is_low)
    def _():
        spread_half(0, all_rows)
        for high in (1, 0):
            for mask in (3, 2, 1, 0):
                spread_to(1, high * side + flip(near, mask), kept_rows[high])
    @pl.when(is_high)
    def _():
        for high in (0, 1):
            for mask in (3, 2, 1, 0):
                spread_to(0, high * side + flip(near, mask), lent_rows[high])

    for high in range(2):

        @pl.when(is_high & (far == high))
        def _():
            for mask in (7, 6, 5, 3, 4, 2, 1):
                peer_high = high if mask < 4 else 1 - high
                spread_to(
                    1, peer_high * side + flip(near, mask % 4), kept_rows[peer_high]
                )


    vertex_rows[own] = hidden_two[rank]

    groups = vert_dev // SUBLANES
    group_rows = half_snaps * SUBLANES
    pair = 2 * group_rows
    pair_dims = 2 * head_dim
    quads = width // LANES
    quad_pairs = LANES // pair_dims
    half_dev = n_snap // 2

    def split(array):
        array = array.reshape(half_snaps, -1, SUBLANES, width)
        return [array[:, at].reshape(group_rows, width) for at in range(array.shape[1])]

    def project(flat, at):
        return split(jnp.dot(flat, weights[at], preferred_element_type=jnp.float32))

    def score(keys, turned):
        keys = keys.astype(jnp.bfloat16)
        return [
            jnp.dot(
                keys[:, at * LANES : (at + 1) * LANES],
                turned[at],
                preferred_element_type=jnp.float32,
            )
            for at in range(quads)
        ]

    quad_columns = quad_pairs * pair
    row_at = lax.broadcasted_iota(jnp.int32, (group_rows, quad_columns), 0)
    col_at = lax.broadcasted_iota(jnp.int32, (group_rows, quad_columns), 1) % group_rows
    same = row_at % SUBLANES == col_at % SUBLANES
    visible = same & (row_at // SUBLANES <= col_at // SUBLANES)
    factor = head_dim ** (-0.5) * math.log2(math.e)
    none = jnp.zeros((pair_dims, pair), jnp.bfloat16)
    ones = jnp.ones((2 * SUBLANES, group_rows), jnp.bfloat16)

    def masked(keys, queries, seen):
        return [jnp.where(seen, each, masked_score) for each in score(keys, queries)]

    def turn(listed):
        doubled = jnp.concatenate([query for query in listed for _ in range(2)], axis=0)
        turned = jnp.transpose(doubled.astype(jnp.bfloat16))
        turned_head = lax.broadcasted_iota(jnp.int32, turned.shape, 0) // head_dim
        turned_side = lax.broadcasted_iota(jnp.int32, turned.shape, 1) // group_rows
        turned = jnp.where(turned_head % 2 == turned_side % 2, turned, 0.0)
        queries = []
        for at in range(len(listed)):
            columns = turned[:, at * pair : (at + 1) * pair]
            pairs = [
                columns[first : first + pair_dims] for first in range(0, width, pair_dims)
            ]
            queries.append(
                [
                    jnp.concatenate(
                        [
                            jnp.concatenate(
                                [
                                    pairs[quad * quad_pairs + inner] if inner == outer else none
                                    for inner in range(quad_pairs)
                                ],
                                axis=0,
                            )
                            for outer in range(quad_pairs)
                        ],
                        axis=1,
                    )
                    for quad in range(quads)
                ]
            )
        return queries

    def attend(scores_of, values_of, before):
        lane_odd = lax.broadcasted_iota(jnp.int32, (group_rows, width), 1) // head_dim % 2 == 1
        count = len(before)
        contexts = []
        for at in range(count):
            value = jnp.transpose(
                jnp.concatenate([each[at] for each in values_of], axis=0).astype(jnp.bfloat16)
            )
            tail = jnp.concatenate([ones] * len(values_of), axis=1)
            context = []
            for quad in range(quads):
                listed = [each[at][quad] for each in scores_of]
                highest = functools.reduce(
                    jnp.maximum, [jnp.max(each, axis=0, keepdims=True) for each in listed]
                )
                shares = jnp.concatenate(
                    [
                        jnp.exp2((each - highest) * factor).astype(jnp.bfloat16)
                        for each in listed
                    ],
                    axis=0,
                )
                for inner in range(quad_pairs):
                    first = (quad * quad_pairs + inner) * pair_dims
                    product = jnp.dot(
                        jnp.concatenate([value[first : first + pair_dims], tail], axis=0),
                        shares[:, inner * pair : (inner + 1) * pair],
                        preferred_element_type=jnp.float32,
                    )
                    scale = 1.0 / product[pair_dims : pair_dims + 1]
                    context.append((product[:pair_dims] * scale).astype(jnp.bfloat16))
            context = jnp.transpose(jnp.concatenate(context, axis=0))
            contexts.append(jnp.where(lane_odd, context[group_rows:], context[:group_rows]))
        mixed = jnp.dot(
            jnp.concatenate(contexts, axis=0), weights[5], preferred_element_type=jnp.float32
        ).reshape(count, group_rows, width)
        verts = count * SUBLANES
        evolved = jnp.concatenate(
            [
                (before[at] + mixed[at]).reshape(half_snaps, 1, SUBLANES, width)
                for at in range(count)
            ],
            axis=1,
        ).reshape(half_dev, snap_dev, verts, width)
        low = lax.broadcasted_iota(jnp.int32, (half_dev * verts, LANES), 1) < feat_width
        outs = []
        for at in range(0, n_feat, 2):
            lanes = slice(at * feat_width, (at + 2) * feat_width)
            first = evolved[:, 0, :, lanes].reshape(half_dev * verts, LANES)
            second = evolved[:, 1, :, lanes].reshape(half_dev * verts, LANES)
            even = jnp.where(low, first, pltpu.roll(second, feat_width, 1))
            odd = jnp.where(low, pltpu.roll(first, feat_width, 1), second)
            outs += [each.reshape(half_dev, verts, LANES) for each in (even, odd)]
        return outs

    total = half_dev * n_feat
    outgoing_rows = outgoing.reshape(total * vert_dev, LANES)
    me = (me_snap % half_dev) * n_feat + me_feat

    def hand_back(source, target_half, peer, rows, source_rows, at):
        pltpu.make_async_remote_copy(
            src_ref=source.at[peer % n_feat, peer // n_feat, source_rows],
            dst_ref=returned.at[part, rank, rows],
            send_sem=return_send.at[at],
            recv_sem=return_recv.at[at],
            device_id=(target_half * half_dev + peer // n_feat, peer % n_feat),
            device_id_type=MESH,
        ).start()

    masks = (14, 15, 12, 13, 10, 11, 6, 7, 8, 9, 4, 5, 2, 3, 1, 0)
    mirrored = [
        flip(me // 2, mask // 2) * 2 + (1 - me % 2 if mask % 2 else me % 2) for mask in masks
    ]

    def own_part(rows):
        flat = rows.reshape(half_snaps * vert_dev, width)
        return project(flat, 2), project(flat, 3), project(flat, 4), split(flat.astype(jnp.float32))

    @pl.when(is_low)
    def _():
        settle(vertex_rows.at[pl.ds(0, half_snaps - 1)], spread_recv.at[0])
        queries, keys, values, before = own_part(vertex_rows[pl.ds(0, half_snaps)])
        queries = turn(queries)
        scores = [masked(keys[at], queries[at], visible) for at in range(groups)]
        for at, out in enumerate(attend([scores], [values], before)):
            outgoing[at] = out.astype(jnp.bfloat16)
        for peer in mirrored[:-1]:
            hand_back(outgoing, 0, peer, all_rows, all_rows, 0)
        load(outgoing.at[me_feat, me_snap % half_dev], returned.at[part, rank], 0)
        for high in range(2):

            @pl.when(far == high)
            def _():
                count = LENT[high]
                settle(
                    vertex_rows.at[pl.ds(0, half_snaps), lent_rows[high]], spread_recv.at[1]
                )
                base = keeps[high] // (2 * SUBLANES) * 2 * SUBLANES
                lent = vertex_rows[
                    pl.ds(half_snaps, half_snaps), pl.ds(base, vert_dev - base)
                ].astype(jnp.float32)[:, keeps[high] - base :]
                flats = split(lent)
                rounded = jnp.concatenate(flats, axis=0).astype(jnp.bfloat16)

                def lent_part(at):
                    out = jnp.dot(rounded, weights[at], preferred_element_type=jnp.float32)
                    return [
                        out[each * group_rows : (each + 1) * group_rows]
                        for each in range(count)
                    ]

                turned = turn(lent_part(2))
                lent_keys = lent_part(3)
                scores = [masked(lent_keys[at], turned[at], visible) for at in range(count)]
                scores_low = [
                    masked(keys[groups - count + at], turned[at], same)
                    for at in range(count)
                ]
                outs = attend(
                    [scores_low, scores], [values[groups - count :], lent_part(4)], flats
                )
                for at, out in enumerate(outs):
                    lending[at, :, pl.ds(0, lends[high])] = out.astype(jnp.bfloat16)
                for peer in mirrored:
                    hand_back(lending, 1, peer, lent_rows[high], pl.ds(0, lends[high]), 1)
                settle(outgoing_rows.at[pl.ds(0, total * lends[high])], return_send.at[1])

        settle(hidden_one.at[pl.ds(0, side * sum(keeps))], spread_send.at[1])
        settle(hidden_two.at[pl.ds(0, half_snaps - 1)], spread_send.at[0])
        pltpu.make_async_copy(
            outgoing.at[0, 0], returned.at[part, rank], load_sem.at[0]
        ).wait()
        everyone = outgoing_rows.at[pl.ds(0, (total - 1) * vert_dev)]
        settle(everyone, return_recv.at[0])
        settle(everyone, return_send.at[0])

    for high in range(2):

        @pl.when(is_high & (far == high))
        def _():
            keep = keeps[high]
            count = groups - LENT[high]
            kept = kept_rows[high]
            settle(vertex_rows.at[pl.ds(0, half_snaps - 1), kept], spread_recv.at[1])
            queries, keys, values, before = own_part(
                vertex_rows[pl.ds(half_snaps, half_snaps)]
            )
            queries = turn(queries[:count])
            scores = [masked(keys[at], queries[at], visible) for at in range(count)]
            settle(vertex_rows.at[pl.ds(0, half_snaps), kept], spread_recv.at[0])
            flat_low = vertex_rows[pl.ds(0, half_snaps)].reshape(half_snaps * vert_dev, width)
            keys_low, values_low = project(flat_low, 3), project(flat_low, 4)
            scores_low = [masked(keys_low[at], queries[at], same) for at in range(count)]
            outs = attend([scores_low, scores], [values_low, values], before[:count])
            for at, out in enumerate(outs):
                outgoing[at, :, kept] = out.astype(jnp.bfloat16)
            for peer in mirrored[:-1]:
                hand_back(outgoing, 1, peer, kept, kept, 0)
            own_copy = load(
                outgoing.at[me_feat, me_snap % half_dev, kept], returned.at[part, rank, kept], 0
            )
            settle(hidden_one.at[pl.ds(0, side * sum(lends))], spread_send.at[0])
            settle(
                hidden_one.at[pl.ds(0, side * sum(keeps) - keep)], spread_send.at[1]
            )
            own_copy.wait()
            settle(
                outgoing_rows.at[pl.ds(0, total // 2 * sum(keeps) - keep)], return_recv.at[0]
            )
            settle(
                outgoing_rows.at[pl.ds(0, total // 2 * sum(lends))], return_recv.at[1]
            )
            settle(outgoing_rows.at[pl.ds(0, (total - 1) * keep)], return_send.at[0])

    settle(pieces.at[pl.ds(0, n_feat - 1)], gather_send)


def on_device_fused(n_snap, n_feat, *operands):
    node_features, _, _, _, tile_values, layer_one = operands[:6]
    snap_dev, vert_count, feat_width = node_features.shape
    _, slot_total, tile_side, _ = tile_values.shape
    width = layer_one.shape[0]
    parts = n_feat // snap_dev
    snaps = n_snap * snap_dev
    half_snaps = snaps // 2
    vert_dev = vert_count // (parts * half_snaps)
    kept = jnp.bfloat16
    result = pl.pallas_call(
        functools.partial(fused_kernel, n_snap, n_feat),
        out_shape=pltpu.VMEM((parts, half_snaps, vert_dev, LANES), kept),
        in_specs=[pl.BlockSpec(memory_space=pltpu.HBM)] * 11,
        out_specs=pl.BlockSpec(memory_space=pltpu.VMEM),
        scratch_shapes=[
            pltpu.VMEM((slot_total, tile_side, tile_side), kept),
            pltpu.VMEM((6, width, width), kept),
            pltpu.VMEM((feat_width, vert_count), kept),
            pltpu.VMEM((n_feat, feat_width, vert_count), kept),
            pltpu.VMEM((vert_count, vert_count), kept),
            pltpu.VMEM((vert_count, width), kept),
            pltpu.VMEM((vert_count, width), kept),
            pltpu.VMEM((half_snaps, vert_dev, width), kept),
            pltpu.VMEM((snaps, vert_dev, width), kept),
            pltpu.VMEM((n_feat, n_snap // 2, vert_dev, LANES), kept),
            pltpu.VMEM((n_feat, n_snap // 2, max(LENT) * SUBLANES, LANES), kept),
            pltpu.SemaphoreType.DMA((7,)),
            pltpu.SemaphoreType.DMA,
            pltpu.SemaphoreType.DMA((CHUNKS + 1,)),
            pltpu.SemaphoreType.DMA((2,)),
            pltpu.SemaphoreType.DMA((2,)),
            pltpu.SemaphoreType.DMA((2,)),
            pltpu.SemaphoreType.DMA((2,)),
            pltpu.SemaphoreType.REGULAR((n_snap // 2,)),
            pltpu.SMEM((snap_dev, slot_total), jnp.int32),
            pltpu.SMEM((snap_dev, slot_total), jnp.int32),
            pltpu.SMEM((snap_dev,), jnp.int32),
        ],
        compiler_params=pltpu.CompilerParams(collective_id=0, has_side_effects=True),
    )(*operands[1:4], node_features.transpose(0, 2, 1), *operands[4:])
    result = jnp.transpose(result.reshape(vert_count, LANES))
    return result.reshape(snap_dev, feat_width, vert_count).transpose(0, 2, 1)


def dispatch(n_snap, n_feat, *operands):
    snap_dev, vert_count, feat_width = operands[0].shape
    slot_total = operands[4].shape[1]
    snaps = n_snap * snap_dev
    fits = (
        snap_dev == 2
        and 2 * feat_width == LANES
        and n_feat == 2 * snap_dev
        and n_snap >= 8
        and n_snap % 4 == 0
        and vert_count % (n_feat // snap_dev * snaps * SUBLANES) == 0
        and snaps * SUBLANES == LANES
        and vert_count >= 4 * SUBLANES * snaps
        and slot_total <= 16
        and vert_count <= 1024
    )
    if fits:
        return on_device_fused(n_snap, n_feat, *operands)
    return on_device(*operands)


def solution(mesh):
    placed = (
        P("snap", None, "feat"),
        P("snap", None),
        P("snap", None),
        P("snap"),
        P("snap", None, None, None),
        P(),
        P(),
        P(),
        P(),
        P(),
        P(),
    )
    return jax.shard_map(
        functools.partial(dispatch, mesh.shape["snap"], mesh.shape["feat"]), mesh=mesh, in_specs=placed, out_specs=P("snap", None, "feat"), check_vma=False
    )
```
